256 devices in a mesh: grp: 4 (over y_hi, core), fsdp: 64 (over y_lo, x, z).
Axes of the slice: x: 4, y: 4 (y_hi: 2, y_lo: 2; y = y_hi * 2 + y_lo), z: 8, core: 2. Of those that a mesh axis runs over, the one named last changes fastest.
Arguments:
- traj_hidden: bfloat16 [262144, 4096], P(('grp', 'fsdp')), may hold values from -24 to 24
- traj_tokens: int32 [262144], P(('grp', 'fsdp')), may hold values from 0 to 511
- traj_action: int32 [262144], P(('grp', 'fsdp')), may hold values from 0 to 511
- traj_return: float32 [262144], P(('grp', 'fsdp')), may hold values from -6 to 6
- traj_episode: int32 [256, 1024], P(('grp', 'fsdp')), may hold values from 0 to 7, never falling along the last dimension, each value on 1 to 512 neighbouring positions
- roll_hidden: bfloat16 [16384, 4096], P(('grp', 'fsdp')), may hold values from -6 to 6
- roll_tokens: int32 [16384], P(('grp', 'fsdp')), may hold values from 0 to 511
- roll_action: int32 [16384], P(('grp', 'fsdp')), may hold values from 0 to 511
- station_table: bfloat16 [512, 4096], replicated, may hold values from -3 to 3
- norm_gain: float32 [4096], replicated, may hold values from 0.7 to 3.9
- head_weight: bfloat16 [4096, 512], P('fsdp'), may hold values from -6 to 6
Outputs:
- new_head: bfloat16 [4096, 512], P('fsdp')
- action_logp: float32 [16384], P(('grp', 'fsdp'))
- episode_logp: float32 [256], P(('grp', 'fsdp'))
The draws below stay inside these ranges and needn't reach their ends.
Inputs may be any that keep to these rules, and one draw needn't show every extreme that they name: `traj_episode`: within each block of 1024 tokens the episode numbers never fall and every number 0 to 7 occurs.
All inputs are finite; a program needn't handle non-finite values.
Results may differ from the reference program's by a relative error of at most 0.0034.
Values may be sent and summed in bfloat16 or wider, within the bound.
A program may use at most 64 MiB of HBM per device.

```python
import math
import jax
import jax.numpy as jnp
import numpy as np
from jax import lax

D = 4096
ACTIONS = 512
STATIONS = 512
TOKL = 1024
EPI_BLK = 8
STEPS = 64
NBLK = 256
LROWS = 262144
RROWS = 16384


def draw_norm_gain(key, part):
    place = jnp.arange(D, dtype=jnp.float32) / D
    spread = jax.random.uniform(key, (D,), jnp.float32, 0.7, 1.3)
    return spread * jnp.sqrt(1.0 + 2.0 * place)


def draw_head_weight(key, part):
    base = jax.random.normal(jax.random.fold_in(key, 11), (D, ACTIONS), jnp.float32) / math.sqrt(D)
    return jnp.clip(base, -6.0, 6.0).astype(jnp.bfloat16)


def plant(values, key, least, top_value):
    spot = [jax.random.randint(jax.random.fold_in(key, axis), (), 0, length) for axis, length in enumerate(values.shape)]
    widest = values.shape.index(max(values.shape))
    beside = spot[:widest] + [(spot[widest] + 1) % values.shape[widest]] + spot[widest + 1:]
    return values.at[tuple(spot)].set(least).at[tuple(beside)].set(top_value)


def raised(entries, own_key, source, target, parts, factor):
    owner, partner = [(jnp.arange(entries.shape[position]) // (entries.shape[position] // parts)).reshape([-1 if axis == position else 1 for axis in range(entries.ndim)]) for position in (source, target)]
    chosen = jax.random.permutation(own_key, parts)[partner]
    strong = (owner == chosen) | (owner == (partner + parts // 2) % parts)
    return jnp.where(strong, factor * entries, entries)


def shard_levels(rng, extent, shards, low, high):
    def one(axis_at, parts):
        heights = jax.random.uniform(jax.random.fold_in(jax.random.fold_in(rng, 6), axis_at), (parts,), jnp.float32, low / len(shards), high / len(shards))
        return jnp.repeat(jnp.exp(heights), extent[axis_at] // parts).reshape((-1,) + (1,) * (len(extent) - axis_at - 1))

    level = one(*shards[0])
    for cut in shards[1:]:
        level = level * one(*cut)
    return level


def rank_bounds(number_of, skew):
    portions = [(1 << 20) // math.isqrt(grade ** skew) + 1 for grade in range(1, number_of + 1)]
    scale = 1 + sum(portions) // (1 << 30)
    return np.cumsum(np.array([max(1, weight // scale) for weight in portions]))


def skewed_ids(own_key, extent, number_of, skew):
    grid = rank_bounds(number_of, skew)
    ticket = jax.random.randint(jax.random.fold_in(own_key, 1), extent, 0, int(grid[number_of - 1]))
    grade = jnp.searchsorted(jnp.asarray(grid, jnp.int32), ticket, side="right")
    return jax.random.permutation(jax.random.fold_in(own_key, 2), number_of)[grade].astype(jnp.int32)


def length_profile(amount, total, bound, slope):
    loads = [(1 << 20) // math.isqrt(grade ** slope) + 1 for grade in range(2, amount + 1)]
    surplus, given = total - bound - (amount - 1), [1] * (amount - 1)
    while surplus > 0:
        candidates = [i for i in range(amount - 1) if given[i] < bound]
        pool, remaining = sum([loads[i] for i in candidates]), surplus
        for i in candidates:
            addition = min(bound - given[i], max(1, remaining * loads[i] // pool), surplus)
            given[i] = given[i] + addition
            surplus = surplus - addition
    return np.array([bound] + given)


def ragged_sizes(stream_key, amount, total, most, lean):
    if amount == 2:
        one = jax.random.randint(stream_key, (), max(1, total - most), min(most, total - 1) + 1)
        return jnp.stack([one, total - one])
    lengths = jnp.asarray(length_profile(amount, total, most, lean), jnp.int32)
    twos = (amount - 1) // 2
    giver, receiver = lengths[1:1 + 2 * twos:2], lengths[2:2 + 2 * twos:2]
    margin = jnp.minimum(giver - 1, most - receiver)
    shifted = jax.random.randint(jax.random.fold_in(stream_key, 1), (twos,), 0, 1 << 20) % (margin + 1)
    lengths = lengths.at[1:1 + 2 * twos:2].set(giver - shifted).at[2:2 + 2 * twos:2].set(receiver + shifted)
    return lengths[jax.random.permutation(jax.random.fold_in(stream_key, 2), amount)]


def scatter_about(key, extent, scale, bound, pieces=(), kind=jnp.bfloat16):
    array = scale * jax.random.normal(key, extent, jnp.float32)
    if pieces:
        array = array * shard_levels(key, extent, pieces, -0.22, 0.18)
    return jnp.clip(array, -bound, bound).astype(kind)


def gaussian_with(own_key, dims, width, most, cuts, heavy, kind=jnp.bfloat16):
    entries = width * jax.random.normal(own_key, dims, jnp.float32)
    if cuts:
        entries = entries * shard_levels(own_key, dims, cuts, -0.22, 0.18)
    return jnp.clip(raised(entries, jax.random.fold_in(own_key, 3), *heavy), -most, most).astype(kind)


def setup_inputs(seed: int = 0) -> dict:
    key_list = jax.random.split(jax.random.key(seed), 12)
    traj_hidden = gaussian_with(key_list[0], (LROWS, D), 1.0, 24.0, ((0, 256),), (0, 1, 256, 6.0))
    traj_tokens = plant(skewed_ids(key_list[1], (LROWS,), STATIONS, 2), jax.random.fold_in(key_list[1], 3), 0, STATIONS - 1).astype(jnp.int32)
    traj_action = plant(jax.random.randint(key_list[2], (LROWS,), 0, ACTIONS), jax.random.fold_in(key_list[2], 1), 0, ACTIONS - 1).astype(jnp.int32)
    traj_return = scatter_about(key_list[3], (LROWS,), 1.0, 6.0, ((0, 256),), jnp.float32)
    traj_episode = jax.vmap(lambda own: jnp.searchsorted(jnp.cumsum(ragged_sizes(own, EPI_BLK, TOKL, TOKL // 2, 1)), jnp.arange(TOKL), side="right"))(jax.random.split(key_list[4], NBLK)).reshape((NBLK, TOKL)).astype(jnp.int32)
    roll_hidden = scatter_about(key_list[5], (RROWS, D), 1.0, 6.0, ((0, 256),))
    roll_tokens = plant(skewed_ids(key_list[6], (RROWS,), STATIONS, 2), jax.random.fold_in(key_list[6], 3), 0, STATIONS - 1).astype(jnp.int32)
    roll_action = plant(jax.random.randint(key_list[7], (RROWS,), 0, ACTIONS), jax.random.fold_in(key_list[7], 1), 0, ACTIONS - 1).astype(jnp.int32)
    station_table = scatter_about(key_list[8], (STATIONS, D), 0.5, 3.0)
    norm_gain = draw_norm_gain(jax.random.fold_in(key_list[11], 71), 0)
    head_weight = draw_head_weight(jax.random.fold_in(key_list[11], 71), 0)
    return {"traj_hidden": traj_hidden, "traj_tokens": traj_tokens, "traj_action": traj_action, "traj_return": traj_return, "traj_episode": traj_episode, "roll_hidden": roll_hidden, "roll_tokens": roll_tokens, "roll_action": roll_action, "station_table": station_table, "norm_gain": norm_gain, "head_weight": head_weight}


step_length = 8.0

def station_rows(hidden, tokens, table, gain):
    mixed = hidden.astype(jnp.float32) + table[tokens].astype(jnp.float32)
    power = lax.optimization_barrier(jnp.mean(mixed * mixed, axis=-1, keepdims=True))
    return (mixed * lax.rsqrt(power + 1e-05) * gain).astype(jnp.bfloat16)

def product(left, right):
    return jnp.dot(left.astype(jnp.float32), right.astype(jnp.float32), precision=lax.Precision.HIGHEST)

def picked_logp(logits, actions):
    top = lax.optimization_barrier(jnp.max(logits, axis=-1, keepdims=True))
    total = jnp.log(lax.optimization_barrier(jnp.sum(jnp.exp(logits - top), axis=-1))) + top[:, 0]
    chosen = (actions[:, None] == jnp.arange(ACTIONS, dtype=jnp.int32)[None, :]).astype(jnp.float32)
    return lax.optimization_barrier(jnp.sum(logits * chosen, axis=-1)) - total

def reference(traj_hidden, traj_tokens, traj_action, traj_return, traj_episode, roll_hidden, roll_tokens, roll_action, station_table, norm_gain, head_weight):
    features = station_rows(traj_hidden, traj_tokens, station_table, norm_gain)
    logits = product(features, head_weight)
    top = lax.optimization_barrier(jnp.max(logits, axis=-1, keepdims=True))
    expo = jnp.exp(logits - top)
    probs = expo / lax.optimization_barrier(jnp.sum(expo, axis=-1, keepdims=True))
    member = (traj_episode[:, :, None] == jnp.arange(EPI_BLK, dtype=jnp.int32)[None, None, :]).astype(jnp.float32)
    returns = traj_return.reshape(traj_episode.shape)
    sums = jnp.einsum('bte,bt->be', member, returns, precision=lax.Precision.HIGHEST)
    counts = lax.optimization_barrier(jnp.sum(member, axis=1))
    baseline = jnp.einsum('bte,be->bt', member, sums / counts, precision=lax.Precision.HIGHEST).reshape(-1)
    advantage = traj_return - baseline
    chosen = (traj_action[:, None] == jnp.arange(ACTIONS, dtype=jnp.int32)[None, :]).astype(jnp.float32)
    scores = (advantage[:, None] * (probs - chosen)).astype(jnp.bfloat16)
    grad = jnp.dot(features.astype(jnp.float32).T, scores.astype(jnp.float32), precision=lax.Precision.HIGHEST)
    gnorm = jnp.sqrt(jnp.sum(grad * grad) + 1e-06)
    new_head = (head_weight.astype(jnp.float32) - step_length * grad / gnorm).astype(jnp.bfloat16)
    rollout = station_rows(roll_hidden, roll_tokens, station_table, norm_gain)
    roll_logits = product(rollout, new_head)
    action_logp = picked_logp(roll_logits, roll_action)
    episode_logp = lax.optimization_barrier(jnp.sum(action_logp.reshape(-1, STEPS), axis=1))
    return (new_head, action_logp, episode_logp)
```

```python
import functools
import itertools

import jax
import jax.numpy as jnp
from jax import lax
from jax.experimental import pallas as pl
from jax.experimental.pallas import tpu as pltpu
from jax.sharding import PartitionSpec as P

ACTIONS = 512
STATIONS = 512
EPI_BLK = 8
STEPS = 64
D = 4096
MESH = pl.DeviceIdType.MESH
NY, NX, NZ = 4, 4, 8
ROWS = 32
HALF = 256
PART = 128

step_length = 8.0


def station_rows(hidden, tokens, table, gain):
    lookup = (tokens[:, None] == jnp.arange(STATIONS, dtype=jnp.int32)[None, :]).astype(
        jnp.bfloat16
    )
    embedded = jnp.dot(lookup, table, preferred_element_type=jnp.float32)
    mixed = hidden.astype(jnp.float32) + embedded
    power = jnp.mean(mixed * mixed, axis=-1, keepdims=True)
    return (mixed * lax.rsqrt(power + 1e-05) * gain).astype(jnp.bfloat16)


def add_columns(left, piece):
    return jnp.dot(left, piece, preferred_element_type=jnp.float32)


def picked_logp(logits, actions):
    top = jnp.max(logits, axis=-1, keepdims=True)
    total = jnp.log(jnp.sum(jnp.exp(logits - top), axis=-1)) + top[:, 0]
    chosen = (actions[:, None] == jnp.arange(ACTIONS, dtype=jnp.int32)[None, :]).astype(jnp.float32)
    return jnp.sum(logits * chosen, axis=-1) - total


def episode_advantage(returns, episode):
    member = (episode[:, None] == jnp.arange(EPI_BLK, dtype=jnp.int32)[None, :]).astype(jnp.float32)
    sums = jnp.dot(member.T, returns, precision=lax.Precision.HIGHEST)
    counts = jnp.sum(member, axis=0)
    baseline = jnp.dot(member, sums / counts, precision=lax.Precision.HIGHEST)
    return returns - baseline


def outer_rows(left, right):
    return lax.dot_general(
        left, right, (((0,), (0,)), ((), ())), preferred_element_type=jnp.float32
    )


class Place:
    def __init__(self):
        grp, shard = lax.axis_index("grp"), lax.axis_index("fsdp")
        self.core = lax.rem(grp, 2)
        self.y = lax.div(grp, 2) * 2 + lax.div(shard, 32)
        self.x = lax.rem(lax.div(shard, 8), 4)
        self.z = lax.rem(shard, 8)
        self.y_hi = lax.div(grp, 2)
        self.shard = shard

    def at(self, y=None, x=None, z=None, core=None):
        y = self.y if y is None else y
        x = self.x if x is None else x
        z = self.z if z is None else z
        core = self.core if core is None else core
        return (lax.div(y, 2) * 2 + core, lax.rem(y, 2) * 32 + x * 8 + z)

    def sibling(self):
        return self.at(core=1 - self.core)

    def along_z(self, k):
        return self.at(z=lax.rem(self.z + k, NZ))

    def along_y(self, k):
        return self.at(y=lax.rem(self.y + k, NY))

    def along_x(self, k):
        return self.at(x=lax.rem(self.x + k, NX))


def greet(here):
    barrier = pltpu.get_barrier_semaphore()
    friends = [here.along_z(k) for k in range(1, NZ)]
    friends += [here.along_y(1), here.along_y(3), here.along_x(1), here.along_x(3)]
    friends += [here.sibling()]
    for friend in friends:
        pl.semaphore_signal(barrier, inc=1, device_id=friend, device_id_type=MESH)
    pl.semaphore_wait(barrier, len(friends))


def send(src, dst, sems, index, device):
    copy = pltpu.make_async_remote_copy(
        src_ref=src,
        dst_ref=dst,
        send_sem=sems[0].at[index],
        recv_sem=sems[1].at[index],
        device_id=device,
        device_id_type=MESH,
    )
    copy.start()
    return copy


def together(*walks):
    for _ in itertools.zip_longest(*walks):
        pass


GATHER_SEMS = 7 + 6 + 6 + 8


def gather_part(buf, first, second, along_first, along_second, here, sems, base):
    core, z = here.core, here.z
    sends = []
    mine = buf.at[core, second, first, z]
    for k in range(1, NZ):
        sends.append(send(mine, mine, sems, base + k - 1, here.along_z(k)))
    yield
    for copy in sends[-7:]:
        copy.wait_recv()
    base += 7

    def ring(view, me, along, base, arrived):
        plus, minus = along(1), along(3)
        after, opposite, before = lax.rem(me + 1, 4), lax.rem(me + 2, 4), lax.rem(me + 3, 4)
        h0, h1 = view(me, 0), view(me, 1)
        c = [
            send(h0, h0, sems, base + 0, plus),
            send(h1, h1, sems, base + 1, minus),
            send(h1, h1, sems, base + 2, plus),
            send(h0, h0, sems, base + 3, minus),
        ]
        arrived(me, 0)
        arrived(me, 1)
        yield
        c[0].wait_recv()
        onward = view(before, 0)
        c.append(send(onward, onward, sems, base + 4, plus))
        arrived(before, 0)
        yield
        c[1].wait_recv()
        onward = view(after, 1)
        c.append(send(onward, onward, sems, base + 5, minus))
        arrived(after, 1)
        yield
        c[2].wait_recv()
        arrived(before, 1)
        yield
        c[3].wait_recv()
        arrived(after, 0)
        yield
        c[4].wait_recv()
        arrived(opposite, 0)
        yield
        c[5].wait_recv()
        arrived(opposite, 1)
        sends.extend(c)

    yield from ring(
        lambda b, h: buf.at[core, second, b, pl.ds(4 * h, 4)],
        first,
        along_first,
        base,
        lambda b, h: None,
    )
    base += 6
    outer = lambda b, h: buf.at[core, b, pl.ds(2 * h, 2)]
    shared = []

    def share(b, h):
        shared.append(
            send(outer(b, h), outer(b, h), sems, base + 6 + len(shared), here.sibling())
        )

    yield from ring(outer, second, along_second, base, share)
    yield
    for copy in shared:
        copy.wait_recv()
    for copy in sends + shared:
        copy.wait_send()


def gather(buf_a, buf_b, here, sems):
    together(
        gather_part(buf_a, here.x, here.y, here.along_x, here.along_y, here, sems, 0),
        gather_part(buf_b, here.y, here.x, here.along_y, here.along_x, here, sems, GATHER_SEMS),
    )


SUM_SEMS = 6 + 6 + 7


def sum_part(total, outer, inner, along_outer, along_inner, bufs, here, sems, base):
    out1, in1, out2, in2, out3, in3 = bufs
    sends = []

    def ring(block, me, along, out, come, base):
        plus, minus = along(1), along(3)
        after, opposite, before = lax.rem(me + 1, 4), lax.rem(me + 2, 4), lax.rem(me + 3, 4)

        def post(slot, value, device):
            out[slot] = value.astype(jnp.bfloat16)
            copy = send(out.at[slot], come.at[slot], sems, base + slot, device)
            sends.append(copy)
            return copy

        def got(slot):
            return come[slot].astype(jnp.float32)

        c0 = post(0, block(opposite, 0)[...], plus)
        c1 = post(1, block(opposite, 1)[...], minus)
        c2 = post(2, block(after, 1)[...], plus)
        c3 = post(3, block(before, 0)[...], minus)
        yield
        c0.wait_recv()
        c4 = post(4, block(after, 0)[...] + got(0), plus)
        yield
        c1.wait_recv()
        c5 = post(5, block(before, 1)[...] + got(1), minus)
        yield
        c2.wait_recv()
        c3.wait_recv()
        low, high = block(me, 0), block(me, 1)
        low[...] = low[...] + got(3)
        high[...] = high[...] + got(2)
        yield
        c4.wait_recv()
        low[...] = low[...] + got(4)
        yield
        c5.wait_recv()
        high[...] = high[...] + got(5)

    yield from ring(
        lambda b, h: total.at[b, pl.ds(2 * h, 2)], outer, along_outer, out1, in1, base
    )
    base += 6
    yield from ring(
        lambda b, h: total.at[outer, b, pl.ds(4 * h, 4)], inner, along_inner, out2, in2, base
    )
    base += 6
    last = []
    for k in range(1, NZ):
        peer = lax.rem(here.z + k, NZ)
        out3[k - 1] = total[outer, inner, peer].astype(jnp.bfloat16)
        last.append(
            send(out3.at[k - 1], in3.at[k - 1], sems, base + k - 1, here.along_z(k))
        )
    yield
    for copy in last:
        copy.wait_recv()
    result = total[outer, inner, here.z]
    for k in range(1, NZ):
        result = result + in3[k - 1].astype(jnp.float32)
    total[outer, inner, here.z] = result
    for copy in sends + last:
        copy.wait_send()


def head_kernel(shard_ref, whole_ref, buf_a, buf_b, send_sems, recv_sems):
    here = Place()
    rows = pl.ds(pl.multiple_of(here.y_hi * ROWS, ROWS), ROWS)
    for part, (buf, spot) in enumerate(((buf_a, (here.y, here.x)), (buf_b, (here.x, here.y)))):
        cols = pl.ds(pl.multiple_of(here.core * HALF + part * PART, PART), PART)
        buf[here.core, spot[0], spot[1], here.z] = shard_ref[rows, cols]
    greet(here)
    gather(buf_a, buf_b, here, (send_sems, recv_sems))
    for core, y, x in itertools.product(range(2), range(NY), range(NX)):
        for part, blocks in enumerate((buf_a[core, y, x], buf_b[core, x, y])):
            cols = pl.ds(core * HALF + part * PART, PART)
            whole_ref[y % 2, x, :, y // 2, :, cols] = blocks


def part_buffers():
    bf = jnp.bfloat16
    return [
        pltpu.VMEM((6, 2, NZ, ROWS, PART), bf),
        pltpu.VMEM((6, 2, NZ, ROWS, PART), bf),
        pltpu.VMEM((6, 4, ROWS, PART), bf),
        pltpu.VMEM((6, 4, ROWS, PART), bf),
        pltpu.VMEM((NZ - 1, ROWS, PART), bf),
        pltpu.VMEM((NZ - 1, ROWS, PART), bf),
    ]


def step_kernel(grad_hbm, head_ref, new_ref, grad, out0, in0, total_a, total_b, *rest):
    bufs_a, bufs_b = rest[:6], rest[6:12]
    buf_a, buf_b = rest[12:14]
    load_sem, pair_send, pair_recv, sum_send, sum_recv, all_send, all_recv = rest[14:]
    here = Place()
    load = pltpu.make_async_copy(grad_hbm, grad, load_sem)
    load.start()
    greet(here)
    load.wait()
    own = pl.ds(pl.multiple_of(here.core * HALF, HALF), HALF)
    other = pl.ds(pl.multiple_of((1 - here.core) * HALF, HALF), HALF)
    pairs = []
    for k in range(8):
        rows = pl.ds(512 * k, 512)
        out0[k] = grad[rows, other].astype(jnp.bfloat16)
        pairs.append(send(out0.at[k], in0.at[k], (pair_send, pair_recv), k, here.sibling()))
    for k in range(8):
        pairs[k].wait_recv()
        y_lo, x = k // 4, k % 4
        both = grad[pl.ds(512 * k, 512), own] + in0[k].astype(jnp.float32)
        both = both.reshape(NZ, 2, ROWS, HALF)
        for y_hi in range(2):
            y = 2 * y_hi + y_lo
            total_a[y, x] = both[:, y_hi, :, :PART]
            total_b[x, y] = both[:, y_hi, :, PART:]
    sems = (sum_send, sum_recv)
    together(
        sum_part(total_a, here.y, here.x, here.along_y, here.along_x, bufs_a, here, sems, 0),
        sum_part(
            total_b, here.x, here.y, here.along_x, here.along_y, bufs_b, here, sems, SUM_SEMS
        ),
    )
    buf_a[here.core, here.y, here.x, here.z] = total_a[here.y, here.x, here.z].astype(jnp.bfloat16)
    buf_b[here.core, here.x, here.y, here.z] = total_b[here.x, here.y, here.z].astype(jnp.bfloat16)
    gather(buf_a, buf_b, here, (all_send, all_recv))
    for copy in pairs:
        copy.wait_send()
    squares = jnp.zeros((ROWS, PART), jnp.float32)
    for core, y, x in itertools.product(range(2), range(NY), range(NX)):
        for block in (buf_a[core, y, x], buf_b[core, x, y]):
            block = block.astype(jnp.float32)
            squares = squares + jnp.sum(block * block, axis=0)
    scale = step_length * lax.rsqrt(jnp.sum(squares, keepdims=True) + 1e-06)
    for core, y, x in itertools.product(range(2), range(NY), range(NX)):
        for part, block in enumerate((buf_a[core, y, x], buf_b[core, x, y])):
            cols = pl.ds(core * HALF + part * PART, PART)
            head = head_ref[y % 2, x, :, y // 2, :, cols].astype(jnp.float32)
            step = block.astype(jnp.float32) * scale.reshape(1, 1, 1)
            new_ref[y % 2, x, :, y // 2, :, cols] = (head - step).astype(jnp.bfloat16)


SPREAD = (2, NX, NZ, 2, ROWS, ACTIONS)


def dma_sems(count):
    return [pltpu.SemaphoreType.DMA((count,)), pltpu.SemaphoreType.DMA((count,))]


def gather_buffers():
    return [
        pltpu.VMEM((2, NY, NX, NZ, ROWS, PART), jnp.bfloat16),
        pltpu.VMEM((2, NX, NY, NZ, ROWS, PART), jnp.bfloat16),
    ]


def gather_head(shard):
    return pl.pallas_call(
        head_kernel,
        out_shape=jax.ShapeDtypeStruct(SPREAD, jnp.bfloat16),
        in_specs=[pl.BlockSpec(memory_space=pltpu.VMEM)],
        out_specs=pl.BlockSpec(memory_space=pltpu.VMEM),
        scratch_shapes=gather_buffers() + dma_sems(2 * GATHER_SEMS),
        compiler_params=pltpu.CompilerParams(
            collective_id=0, has_side_effects=True, vmem_limit_bytes=32 << 20
        ),
    )(shard)


def take_step(grad, head):
    return pl.pallas_call(
        step_kernel,
        out_shape=jax.ShapeDtypeStruct(SPREAD, jnp.bfloat16),
        in_specs=[pl.BlockSpec(memory_space=pl.ANY), pl.BlockSpec(memory_space=pltpu.VMEM)],
        out_specs=pl.BlockSpec(memory_space=pltpu.VMEM),
        scratch_shapes=[
            pltpu.VMEM((D, ACTIONS), jnp.float32),
            pltpu.VMEM((8, 512, HALF), jnp.bfloat16),
            pltpu.VMEM((8, 512, HALF), jnp.bfloat16),
            pltpu.VMEM((NY, NX, NZ, ROWS, PART), jnp.float32),
            pltpu.VMEM((NX, NY, NZ, ROWS, PART), jnp.float32),
            *part_buffers(),
            *part_buffers(),
            *gather_buffers(),
            pltpu.SemaphoreType.DMA(()),
            *dma_sems(8),
            *dma_sems(2 * SUM_SEMS),
            *dma_sems(2 * GATHER_SEMS),
        ],
        compiler_params=pltpu.CompilerParams(
            collective_id=1, has_side_effects=True, vmem_limit_bytes=56 << 20
        ),
    )(grad, head)


def local(
    traj_hidden,
    traj_tokens,
    traj_action,
    traj_return,
    traj_episode,
    roll_hidden,
    roll_tokens,
    roll_action,
    station_table,
    norm_gain,
    head_weight,
):
    head = gather_head(head_weight)
    features = station_rows(traj_hidden, traj_tokens, station_table, norm_gain)
    rollout = station_rows(roll_hidden, roll_tokens, station_table, norm_gain)
    advantage = episode_advantage(traj_return, traj_episode[0])
    logits = add_columns(features, head.reshape(D, ACTIONS))
    top = jnp.max(logits, axis=-1, keepdims=True)
    expo = jnp.exp(logits - top)
    probs = expo / jnp.sum(expo, axis=-1, keepdims=True)
    chosen = (traj_action[:, None] == jnp.arange(ACTIONS, dtype=jnp.int32)[None, :]).astype(
        jnp.float32
    )
    scores = (advantage[:, None] * (probs - chosen)).astype(jnp.bfloat16)
    new_whole = take_step(outer_rows(features, scores), head).reshape(D, ACTIONS)
    new_head = lax.dynamic_slice_in_dim(new_whole, lax.axis_index("fsdp") * 64, 64, axis=0)
    roll_logits = add_columns(rollout, new_whole)
    action_logp = picked_logp(roll_logits, roll_action)
    episode_logp = jnp.sum(action_logp.reshape(-1, STEPS), axis=1)
    return (new_head, action_logp, episode_logp)


def solution(mesh):
    placed = (
        P(("grp", "fsdp"), None),
        P(("grp", "fsdp")),
        P(("grp", "fsdp")),
        P(("grp", "fsdp")),
        P(("grp", "fsdp"), None),
        P(("grp", "fsdp"), None),
        P(("grp", "fsdp")),
        P(("grp", "fsdp")),
        P(),
        P(),
        P("fsdp", None),
    )
    return jax.shard_map(
        local,
        mesh=mesh,
        in_specs=placed,
        out_specs=(P("fsdp", None), P(("grp", "fsdp")), P(("grp", "fsdp"))),
        check_vma=False,
    )
```

```python
import itertools

import jax
import jax.numpy as jnp
from jax import lax
from jax.experimental import pallas as pl
from jax.experimental.pallas import tpu as pltpu
from jax.sharding import PartitionSpec as P

ACTIONS = 512
STATIONS = 512
EPI_BLK = 8
STEPS = 64
D = 4096
MESH = pl.DeviceIdType.MESH
NY, NX, NZ = 4, 4, 8
ROWS = 32
HALF = 256
PART = 128

step_length = 8.0


class Place:
    def __init__(self):
        grp, shard = lax.axis_index("grp"), lax.axis_index("fsdp")
        self.core = lax.rem(grp, 2)
        self.y = lax.div(grp, 2) * 2 + lax.div(shard, 32)
        self.x = lax.rem(lax.div(shard, 8), 4)
        self.z = lax.rem(shard, 8)
        self.y_hi = lax.div(grp, 2)
        self.shard = shard

    def at(self, y=None, x=None, z=None, core=None):
        y = self.y if y is None else y
        x = self.x if x is None else x
        z = self.z if z is None else z
        core = self.core if core is None else core
        return (lax.div(y, 2) * 2 + core, lax.rem(y, 2) * 32 + x * 8 + z)

    def sibling(self):
        return self.at(core=1 - self.core)

    def along_z(self, k):
        return self.at(z=lax.rem(self.z + k, NZ))

    def along_y(self, k):
        return self.at(y=lax.rem(self.y + k, NY))

    def along_x(self, k):
        return self.at(x=lax.rem(self.x + k, NX))


def greet(here):
    barrier = pltpu.get_barrier_semaphore()
    friends = [here.along_z(k) for k in range(1, NZ)]
    friends += [here.along_y(1), here.along_y(3), here.along_x(1), here.along_x(3)]
    friends += [here.sibling()]
    for friend in friends:
        pl.semaphore_signal(barrier, inc=1, device_id=friend, device_id_type=MESH)
    pl.semaphore_wait(barrier, len(friends))


def send(src, dst, sems, index, device):
    copy = pltpu.make_async_remote_copy(
        src_ref=src,
        dst_ref=dst,
        send_sem=sems[0].at[index],
        recv_sem=sems[1].at[index],
        device_id=device,
        device_id_type=MESH,
    )
    copy.start()
    return copy


def together(*walks):
    for _ in itertools.zip_longest(*walks):
        pass


GATHER_SEMS = 7 + 6 + 6 + 8


def gather_part(buf, first, second, along_first, along_second, here, sems, base):
    core, z = here.core, here.z
    sends = []
    mine = buf.at[core, second, first, z]
    for k in range(1, NZ):
        sends.append(send(mine, mine, sems, base + k - 1, here.along_z(k)))
    yield
    for copy in sends[-7:]:
        copy.wait_recv()
    base += 7

    def ring(view, me, along, base, arrived):
        plus, minus = along(1), along(3)
        after, opposite, before = lax.rem(me + 1, 4), lax.rem(me + 2, 4), lax.rem(me + 3, 4)
        h0, h1 = view(me, 0), view(me, 1)
        c = [
            send(h0, h0, sems, base + 0, plus),
            send(h1, h1, sems, base + 1, minus),
            send(h1, h1, sems, base + 2, plus),
            send(h0, h0, sems, base + 3, minus),
        ]
        arrived(me, 0)
        arrived(me, 1)
        yield
        c[0].wait_recv()
        onward = view(before, 0)
        c.append(send(onward, onward, sems, base + 4, plus))
        arrived(before, 0)
        yield
        c[1].wait_recv()
        onward = view(after, 1)
        c.append(send(onward, onward, sems, base + 5, minus))
        arrived(after, 1)
        yield
        c[2].wait_recv()
        arrived(before, 1)
        yield
        c[3].wait_recv()
        arrived(after, 0)
        yield
        c[4].wait_recv()
        arrived(opposite, 0)
        yield
        c[5].wait_recv()
        arrived(opposite, 1)
        sends.extend(c)

    yield from ring(
        lambda b, h: buf.at[core, second, b, pl.ds(4 * h, 4)],
        first,
        along_first,
        base,
        lambda b, h: None,
    )
    base += 6
    outer = lambda b, h: buf.at[core, b, pl.ds(2 * h, 2)]
    shared = []

    def share(b, h):
        shared.append(
            send(outer(b, h), outer(b, h), sems, base + 6 + len(shared), here.sibling())
        )

    yield from ring(outer, second, along_second, base, share)
    yield
    for copy in shared:
        copy.wait_recv()
    for copy in sends + shared:
        copy.wait_send()


def gather_walk(buf_a, buf_b, here, sems):
    return itertools.zip_longest(
        gather_part(buf_a, here.x, here.y, here.along_x, here.along_y, here, sems, 0),
        gather_part(buf_b, here.y, here.x, here.along_y, here.along_x, here, sems, GATHER_SEMS),
    )


SUM_SEMS = 6 + 6 + 7


def sum_part(total, outer, inner, along_outer, along_inner, bufs, here, sems, base):
    out1, in1, out2, in2, out3, in3 = bufs
    sends = []

    def ring(block, me, along, out, come, base):
        plus, minus = along(1), along(3)
        after, opposite, before = lax.rem(me + 1, 4), lax.rem(me + 2, 4), lax.rem(me + 3, 4)

        def post(slot, value, device):
            out[slot] = value.astype(jnp.bfloat16)
            copy = send(out.at[slot], come.at[slot], sems, base + slot, device)
            sends.append(copy)
            return copy

        def got(slot):
            return come[slot].astype(jnp.float32)

        c0 = post(0, block(opposite, 0)[...], plus)
        c1 = post(1, block(opposite, 1)[...], minus)
        c2 = post(2, block(after, 1)[...], plus)
        c3 = post(3, block(before, 0)[...], minus)
        yield
        c0.wait_recv()
        c4 = post(4, block(after, 0)[...] + got(0), plus)
        yield
        c1.wait_recv()
        c5 = post(5, block(before, 1)[...] + got(1), minus)
        yield
        c2.wait_recv()
        c3.wait_recv()
        low, high = block(me, 0), block(me, 1)
        low[...] = low[...] + got(3)
        high[...] = high[...] + got(2)
        yield
        c4.wait_recv()
        low[...] = low[...] + got(4)
        yield
        c5.wait_recv()
        high[...] = high[...] + got(5)

    yield from ring(
        lambda b, h: total.at[b, pl.ds(2 * h, 2)], outer, along_outer, out1, in1, base
    )
    base += 6
    yield from ring(
        lambda b, h: total.at[outer, b, pl.ds(4 * h, 4)], inner, along_inner, out2, in2, base
    )
    base += 6
    last = []
    for k in range(1, NZ):
        peer = lax.rem(here.z + k, NZ)
        out3[k - 1] = total[outer, inner, peer].astype(jnp.bfloat16)
        last.append(
            send(out3.at[k - 1], in3.at[k - 1], sems, base + k - 1, here.along_z(k))
        )
    yield
    for copy in last:
        copy.wait_recv()
    result = total[outer, inner, here.z]
    for k in range(1, NZ):
        result = result + in3[k - 1].astype(jnp.float32)
    total[outer, inner, here.z] = result
    for copy in sends + last:
        copy.wait_send()


def part_buffers():
    bf = jnp.bfloat16
    return [
        pltpu.VMEM((6, 2, NZ, ROWS, PART), bf),
        pltpu.VMEM((6, 2, NZ, ROWS, PART), bf),
        pltpu.VMEM((6, 4, ROWS, PART), bf),
        pltpu.VMEM((6, 4, ROWS, PART), bf),
        pltpu.VMEM((NZ - 1, ROWS, PART), bf),
        pltpu.VMEM((NZ - 1, ROWS, PART), bf),
    ]


TILE = 256
WIDE = 1024


def one_hot(column, count):
    spots = lax.broadcasted_iota(jnp.int32, (column.shape[0], count), 1).astype(jnp.float32)
    return column == spots


def columns_of(rows):
    return jnp.transpose(rows)


def advantage_of(returns, episode):
    baseline = jnp.zeros_like(returns)
    for number in range(EPI_BLK):
        member = (episode == number).astype(jnp.float32)
        total = jnp.sum(returns * member, keepdims=True)
        count = jnp.sum(member, keepdims=True)
        baseline = baseline + member * (total / count)
    return returns - baseline


def station_rows(rows_ref, tokens, table, gain, mixed, step):
    n = rows_ref.shape[0]
    lookup = one_hot(tokens, STATIONS).astype(jnp.bfloat16)
    power = jnp.zeros((n, 1), jnp.float32)
    for left in range(0, D, WIDE):
        cols = pl.ds(left, WIDE)
        value = rows_ref[:, cols].astype(jnp.float32) + jnp.dot(
            lookup, table[:, cols], preferred_element_type=jnp.float32
        )
        mixed[:n, cols] = value
        power = power + jnp.sum(value * value, axis=-1, keepdims=True)
        step()
    inverse = lax.rsqrt(power * (1.0 / D) + 1e-05)
    for left in range(0, D, WIDE):
        cols = pl.ds(left, WIDE)
        rows_ref[:, cols] = (mixed[:n, cols] * inverse * gain[:, cols]).astype(jnp.bfloat16)
    step()


def whole_kernel(
    hidden_hbm,
    roll_hbm,
    table_hbm,
    gain,
    ints,
    returns,
    episode,
    shard,
    new_ref,
    logp_ref,
    episode_ref,
    features,
    rollout,
    table,
    mixed,
    scores,
    head,
    out0,
    in0,
    total_a,
    total_b,
    *rest,
):
    bufs_a, bufs_b = rest[:6], rest[6:12]
    head_a, head_b, buf_a, buf_b = rest[12:16]
    load_sem, pair_send, pair_recv, sum_send, sum_recv = rest[16:21]
    head_send, head_recv, all_send, all_recv = rest[21:]
    here = Place()

    loads = [pltpu.make_async_copy(table_hbm, table, load_sem.at[0])]
    tiles = [pl.ds(TILE * i, TILE) for i in range(4)]
    for i, rows in enumerate(tiles):
        loads.append(
            pltpu.make_async_copy(hidden_hbm.at[rows], features.at[rows], load_sem.at[1 + i])
        )
    loads.append(pltpu.make_async_copy(roll_hbm, rollout, load_sem.at[5]))
    for load in loads:
        load.start()

    rows = pl.ds(pl.multiple_of(here.y_hi * ROWS, ROWS), ROWS)
    for part, (buf, spot) in enumerate(((head_a, (here.y, here.x)), (head_b, (here.x, here.y)))):
        cols = pl.ds(pl.multiple_of(here.core * HALF + part * PART, PART), PART)
        buf[here.core, spot[0], spot[1], here.z] = shard[rows, cols]
    greet(here)
    walk = gather_walk(head_a, head_b, here, (head_send, head_recv))
    next(walk)
    turn = itertools.count(1)

    def step():
        if next(turn) % 2 == 0:
            next(walk, None)

    numbers = columns_of(ints[...].astype(jnp.float32))
    advantage = columns_of(advantage_of(returns[...], episode[...]))

    def column(values, first, tile):
        return jnp.concatenate([values[:, first + 2 * tile + j][:, None] for j in range(2)], axis=0)

    loads[0].wait()
    for i, rows in enumerate(tiles):
        loads[1 + i].wait()
        station_rows(features.at[rows], column(numbers, 0, i), table, gain, mixed, step)
    loads[5].wait()
    station_rows(rollout, numbers[:64, 16:17], table, gain, mixed, step)
    for _ in walk:
        pass
    for core, y, x in itertools.product(range(2), range(NY), range(NX)):
        for part, blocks in enumerate((head_a[core, y, x], head_b[core, x, y])):
            head[y % 2, x, :, y // 2, :, pl.ds(core * HALF + part * PART, PART)] = blocks

    for i, rows in enumerate(tiles):
        logits = jnp.dot(
            features[rows, :],
            head[...].reshape(D, ACTIONS),
            preferred_element_type=jnp.float32,
        )
        expo = jnp.exp(logits - jnp.max(logits, axis=-1, keepdims=True))
        probs = expo / jnp.sum(expo, axis=-1, keepdims=True)
        chosen = one_hot(column(numbers, 8, i), ACTIONS).astype(jnp.float32)
        value = (column(advantage, 0, i) * (probs - chosen)).astype(jnp.bfloat16)
        scores[0, rows] = value[:, :HALF]
        scores[1, rows] = value[:, HALF:]

    pairs = []
    mine, theirs = scores[here.core], scores[1 - here.core]
    for k in range(8):
        left = jnp.transpose(features[:, pl.ds(512 * k, 512)])
        out0[k] = jnp.dot(left, theirs, preferred_element_type=jnp.float32).astype(jnp.bfloat16)
        pairs.append(send(out0.at[k], in0.at[k], (pair_send, pair_recv), k, here.sibling()))
        own = jnp.dot(left, mine, preferred_element_type=jnp.float32).reshape(NZ, 2, ROWS, HALF)
        for y_hi in range(2):
            y, x = 2 * y_hi + k // 4, k % 4
            total_a[y, x] = own[:, y_hi, :, :PART]
            total_b[x, y] = own[:, y_hi, :, PART:]
    for k in range(8):
        pairs[k].wait_recv()
        other = in0[k].astype(jnp.float32).reshape(NZ, 2, ROWS, HALF)
        for y_hi in range(2):
            y, x = 2 * y_hi + k // 4, k % 4
            total_a[y, x] = total_a[y, x] + other[:, y_hi, :, :PART]
            total_b[x, y] = total_b[x, y] + other[:, y_hi, :, PART:]

    sems = (sum_send, sum_recv)
    together(
        sum_part(total_a, here.y, here.x, here.along_y, here.along_x, bufs_a, here, sems, 0),
        sum_part(
            total_b, here.x, here.y, here.along_x, here.along_y, bufs_b, here, sems, SUM_SEMS
        ),
    )
    buf_a[here.core, here.y, here.x, here.z] = total_a[here.y, here.x, here.z].astype(jnp.bfloat16)
    buf_b[here.core, here.x, here.y, here.z] = total_b[here.x, here.y, here.z].astype(jnp.bfloat16)
    for _ in gather_walk(buf_a, buf_b, here, (all_send, all_recv)):
        pass
    for copy in pairs:
        copy.wait_send()

    squares = jnp.zeros((ROWS, PART), jnp.float32)
    for core, y, x in itertools.product(range(2), range(NY), range(NX)):
        for block in (buf_a[core, y, x], buf_b[core, x, y]):
            block = block.astype(jnp.float32)
            squares = squares + jnp.sum(block * block, axis=0)
    scale = step_length * lax.rsqrt(jnp.sum(squares, keepdims=True) + 1e-06)
    for core, y, x in itertools.product(range(2), range(NY), range(NX)):
        for part, block in enumerate((buf_a[core, y, x], buf_b[core, x, y])):
            cols = pl.ds(core * HALF + part * PART, PART)
            old = head[y % 2, x, :, y // 2, :, cols].astype(jnp.float32)
            change = block.astype(jnp.float32) * scale.reshape(1, 1, 1)
            head[y % 2, x, :, y // 2, :, cols] = (old - change).astype(jnp.bfloat16)
    new_ref[...] = head[lax.rem(here.y, 2), here.x, here.z].reshape(2 * ROWS, ACTIONS)
    logits = jnp.dot(
        rollout[...], head[...].reshape(D, ACTIONS), preferred_element_type=jnp.float32
    )
    top = jnp.max(logits, axis=-1, keepdims=True)
    total = jnp.log(jnp.sum(jnp.exp(logits - top), axis=-1, keepdims=True)) + top
    chosen = one_hot(numbers[64:, 16:17], ACTIONS).astype(jnp.float32)
    logp = jnp.sum(logits * chosen, axis=-1, keepdims=True) - total
    logp_ref[...] = jnp.transpose(jnp.broadcast_to(logp, (STEPS, 128)))[:1, :]
    episode_ref[...] = jnp.sum(logp, keepdims=True)


SPREAD = (2, NX, NZ, 2, ROWS, ACTIONS)


def dma_sems(count):
    return [pltpu.SemaphoreType.DMA((count,)), pltpu.SemaphoreType.DMA((count,))]


def gather_buffers():
    return [
        pltpu.VMEM((2, NY, NX, NZ, ROWS, PART), jnp.bfloat16),
        pltpu.VMEM((2, NX, NY, NZ, ROWS, PART), jnp.bfloat16),
    ]


def whole_step(hidden, roll, table, gain, ints, returns, episode, shard):
    vmem, anywhere = pl.BlockSpec(memory_space=pltpu.VMEM), pl.BlockSpec(memory_space=pl.ANY)
    return pl.pallas_call(
        whole_kernel,
        out_shape=(
            jax.ShapeDtypeStruct(shard.shape, jnp.bfloat16),
            jax.ShapeDtypeStruct((1, STEPS), jnp.float32),
            jax.ShapeDtypeStruct((1, 1), jnp.float32),
        ),
        in_specs=[anywhere] * 3 + [vmem] * 5,
        out_specs=(vmem, vmem, vmem),
        scratch_shapes=[
            pltpu.VMEM((1024, D), jnp.bfloat16),
            pltpu.VMEM((STEPS, D), jnp.bfloat16),
            pltpu.VMEM((STATIONS, D), jnp.bfloat16),
            pltpu.VMEM((TILE, D), jnp.float32),
            pltpu.VMEM((2, 1024, HALF), jnp.bfloat16),
            pltpu.VMEM(SPREAD, jnp.bfloat16),
            pltpu.VMEM((8, 512, HALF), jnp.bfloat16),
            pltpu.VMEM((8, 512, HALF), jnp.bfloat16),
            pltpu.VMEM((NY, NX, NZ, ROWS, PART), jnp.float32),
            pltpu.VMEM((NX, NY, NZ, ROWS, PART), jnp.float32),
            *part_buffers(),
            *part_buffers(),
            *gather_buffers(),
            *gather_buffers(),
            pltpu.SemaphoreType.DMA((6,)),
            *dma_sems(8),
            *dma_sems(2 * SUM_SEMS),
            *dma_sems(2 * GATHER_SEMS),
            *dma_sems(2 * GATHER_SEMS),
        ],
        compiler_params=pltpu.CompilerParams(
            collective_id=0, has_side_effects=True, vmem_limit_bytes=60 << 20
        ),
    )(hidden, roll, table, gain, ints, returns, episode, shard)


def local(
    traj_hidden,
    traj_tokens,
    traj_action,
    traj_return,
    traj_episode,
    roll_hidden,
    roll_tokens,
    roll_action,
    station_table,
    norm_gain,
    head_weight,
):
    ints = jnp.concatenate([traj_tokens, traj_action, roll_tokens, roll_action]).reshape(17, 128)
    ints = jnp.pad(ints, ((0, 7), (0, 0)))
    new_head, action_logp, episode_logp = whole_step(
        traj_hidden,
        roll_hidden,
        station_table,
        norm_gain.reshape(1, D),
        ints,
        traj_return.reshape(8, 128),
        traj_episode.reshape(8, 128),
        head_weight,
    )
    return (new_head, action_logp.reshape(STEPS), episode_logp.reshape(1))


def solution(mesh):
    placed = (
        P(("grp", "fsdp"), None),
        P(("grp", "fsdp")),
        P(("grp", "fsdp")),
        P(("grp", "fsdp")),
        P(("grp", "fsdp"), None),
        P(("grp", "fsdp"), None),
        P(("grp", "fsdp")),
        P(("grp", "fsdp")),
        P(),
        P(),
        P("fsdp", None),
    )
    return jax.shard_map(
        local,
        mesh=mesh,
        in_specs=placed,
        out_specs=(P("fsdp", None), P(("grp", "fsdp")), P(("grp", "fsdp"))),
        check_vma=False,
    )
```

```python
import itertools

import jax
import jax.numpy as jnp
from jax import lax
from jax.experimental import pallas as pl
from jax.experimental.pallas import tpu as pltpu
from jax.sharding import PartitionSpec as P

ACTIONS = 512
STATIONS = 512
EPI_BLK = 8
STEPS = 64
D = 4096
MESH = pl.DeviceIdType.MESH
NY, NX, NZ = 4, 4, 8
ROWS = 32
HALF = 256
PART = 128

step_length = 8.0


class Place:
    def __init__(self):
        grp, shard = lax.axis_index("grp"), lax.axis_index("fsdp")
        self.core = lax.rem(grp, 2)
        self.y = lax.div(grp, 2) * 2 + lax.div(shard, 32)
        self.x = lax.rem(lax.div(shard, 8), 4)
        self.z = lax.rem(shard, 8)
        self.y_hi = lax.div(grp, 2)
        self.shard = shard

    def at(self, y=None, x=None, z=None, core=None):
        y = self.y if y is None else y
        x = self.x if x is None else x
        z = self.z if z is None else z
        core = self.core if core is None else core
        return (lax.div(y, 2) * 2 + core, lax.rem(y, 2) * 32 + x * 8 + z)

    def sibling(self):
        return self.at(core=1 - self.core)

    def along_z(self, k):
        return self.at(z=lax.rem(self.z + k, NZ))

    def along_y(self, k):
        return self.at(y=lax.rem(self.y + k, NY))

    def along_x(self, k):
        return self.at(x=lax.rem(self.x + k, NX))


def greet(here):
    barrier = pltpu.get_barrier_semaphore()
    friends = [here.along_z(k) for k in range(1, NZ)]
    friends += [here.along_y(k) for k in range(1, NY)] + [here.along_x(k) for k in range(1, NX)]
    friends += [here.sibling()]
    for friend in friends:
        pl.semaphore_signal(barrier, inc=1, device_id=friend, device_id_type=MESH)
    return lambda: pl.semaphore_wait(barrier, len(friends))


def send(src, dst, sems, index, device):
    copy = pltpu.make_async_remote_copy(
        src_ref=src,
        dst_ref=dst,
        send_sem=sems[0].at[index],
        recv_sem=sems[1].at[index],
        device_id=device,
        device_id_type=MESH,
    )
    copy.start()
    return copy


def together(*walks):
    for _ in itertools.zip_longest(*walks):
        pass


GATHER_SEMS = 7 + 3 + 12 + 16


def gather_part(buf, outer, inner, along_outer, along_inner, here, sems, base):
    core, z = here.core, here.z
    numbers = itertools.count(base)
    sends, shared = [], []
    plus, minus = along_outer(1), along_outer(3)

    def put(block, device):
        copy = send(block, block, sems, next(numbers), device)
        sends.append(copy)
        return copy

    def share(block):
        shared.append(send(block, block, sems, next(numbers), here.sibling()))

    def spot(dy, dx):
        return buf.at[core, lax.rem(outer + dy, 4), lax.rem(inner + dx, 4)]

    mine = buf.at[core, outer, inner, z]
    along_z = [put(mine, here.along_z(k)) for k in (1, 7, 2, 6, 3, 5, 4)]
    yield
    for copy in along_z:
        copy.wait_recv()
    inside = {4 - k: put(spot(0, 0), along_inner(k)) for k in (1, 3, 2)}
    up, down = {0: put(spot(0, 0), plus)}, {0: put(spot(0, 0), minus)}
    share(spot(0, 0))
    onward = []

    def spread(k):
        inside[k].wait_recv()
        up[k], down[k] = put(spot(0, k), plus), put(spot(0, k), minus)
        if k == 2:
            onward.append((k, put(spot(0, k), along_outer(2))))
        share(spot(0, k))

    def from_below(k):
        up[k].wait_recv()
        if k in (0, 3):
            onward.append((k, put(spot(3, k), plus)))
        share(spot(3, k))

    def from_above(k):
        down[k].wait_recv()
        if k == 1:
            onward.append((k, put(spot(1, k), minus)))
        share(spot(1, k))

    yield
    spread(1)
    yield
    spread(3)
    yield
    from_below(0)
    yield
    spread(2)
    for k in (1, 3, 2):
        yield
        from_above(k)
        yield
        from_below(k)
    yield
    from_above(0)
    for k, copy in sorted(onward, key=lambda one: one[0] == 2):
        yield
        copy.wait_recv()
        share(spot(2, k))
    yield
    for copy in shared:
        copy.wait_recv()
    for copy in sends + shared:
        copy.wait_send()


def gather_walk(buf_a, buf_b, here, sems):
    return itertools.zip_longest(
        gather_part(buf_a, here.y, here.x, here.along_y, here.along_x, here, sems, 0),
        gather_part(buf_b, here.x, here.y, here.along_x, here.along_y, here, sems, GATHER_SEMS),
    )


SUM_SEMS = 12 + 3 + 7


def sum_part(total, outer, inner, along_outer, along_inner, bufs, here, sems, base):
    out1, in1, out2, in2, out3, in3 = bufs
    plus, minus = along_outer(1), along_outer(3)
    sends = []

    def block(dy, dx):
        return total.at[lax.rem(outer + dy, 4), lax.rem(inner + dx, 4)]

    def post(out, come, slot, value, device, number):
        out[slot] = value.astype(jnp.bfloat16)
        copy = send(out.at[slot], come.at[slot], sems, base + number, device)
        sends.append(copy)
        return copy

    def ring(slot, value, device):
        return post(out1, in1, slot, value, device, slot)

    def got(come, slot):
        return come[slot].astype(jnp.float32)

    order = (2, 1, 3, 0)
    spots = {k: i for i, k in enumerate(order)}
    up, down = (plus, minus, 1, 3), (minus, plus, 3, 1)
    way = {2: up, 0: up, 1: down, 3: down}
    first, direct, last = {}, {}, {}

    def post_first(k):
        first[k] = ring(spots[k], block(2, k)[...], way[k][0])

    def post_direct(k):
        direct[k] = ring(4 + spots[k], block(way[k][3], k)[...], way[k][1])

    inside = {}

    def finish(i, k):
        last[k].wait_recv()
        direct[k].wait_recv()
        value = block(0, k)[...] + got(in1, 4 + i) + got(in1, 8 + i)
        if k == 0:
            block(0, 0)[...] = value
        else:
            inside[k] = post(out2, in2, k - 1, value, along_inner(k), 11 + k)

    def rest():
        for i, k in enumerate(order):
            yield
            first[k].wait_recv()
            last[k] = ring(8 + i, block(way[k][2], k)[...] + got(in1, i), way[k][0])
        for i, k in enumerate(order):
            yield
            finish(i, k)
        for k in (1, 3, 2):
            yield
            inside[k].wait_recv()
            block(0, 0)[...] = block(0, 0)[...] + got(in2, k - 1)
        along_z = []
        for k in (1, 7, 2, 6, 3, 5, 4):
            value = total[outer, inner, lax.rem(here.z + k, NZ)]
            along_z.append((k, post(out3, in3, k - 1, value, here.along_z(k), 14 + k)))
        yield
        value = total[outer, inner, here.z]
        for k, copy in along_z:
            copy.wait_recv()
            value = value + got(in3, k - 1)
        total[outer, inner, here.z] = value
        for copy in sends:
            copy.wait_send()

    return post_first, post_direct, rest


def part_buffers():
    bf = jnp.bfloat16
    return [
        pltpu.VMEM((12, NZ, ROWS, PART), bf),
        pltpu.VMEM((12, NZ, ROWS, PART), bf),
        pltpu.VMEM((3, NZ, ROWS, PART), bf),
        pltpu.VMEM((3, NZ, ROWS, PART), bf),
        pltpu.VMEM((NZ - 1, ROWS, PART), bf),
        pltpu.VMEM((NZ - 1, ROWS, PART), bf),
    ]


TILE = 256
WIDE = 1024


def one_hot(column, count):
    spots = lax.broadcasted_iota(jnp.int32, (column.shape[0], count), 1).astype(jnp.float32)
    return column == spots


def columns_of(rows):
    return jnp.transpose(rows)


def advantage_of(returns, episode):
    baseline = jnp.zeros_like(returns)
    for number in range(EPI_BLK):
        member = (episode == number).astype(jnp.float32)
        total = jnp.sum(returns * member, keepdims=True)
        count = jnp.sum(member, keepdims=True)
        baseline = baseline + member * (total / count)
    return returns - baseline


def station_rows(rows_ref, tokens, table, gain, mixed, step):
    n = rows_ref.shape[0]
    lookup = one_hot(tokens, STATIONS).astype(jnp.bfloat16)
    power = jnp.zeros((n, 1), jnp.float32)
    for left in range(0, D, WIDE):
        cols = pl.ds(left, WIDE)
        value = rows_ref[:, cols].astype(jnp.float32) + jnp.dot(
            lookup, table[:, cols], preferred_element_type=jnp.float32
        )
        mixed[:n, cols] = value
        power = power + jnp.sum(value * value, axis=-1, keepdims=True)
        step()
    inverse = lax.rsqrt(power * (1.0 / D) + 1e-05)
    for left in range(0, D, WIDE):
        cols = pl.ds(left, WIDE)
        rows_ref[:, cols] = (mixed[:n, cols] * inverse * gain[:, cols]).astype(jnp.bfloat16)
    step()


def whole_kernel(
    hidden_hbm,
    roll_hbm,
    table_hbm,
    gain_hbm,
    tokens_hbm,
    action_hbm,
    roll_tokens_hbm,
    roll_action_hbm,
    returns_hbm,
    episode_hbm,
    shard_hbm,
    new_hbm,
    logp_hbm,
    episode_logp_hbm,
    gain,
    ints,
    roll_ints,
    returns,
    episode,
    shard,
    new_ref,
    logp_ref,
    episode_ref,
    features,
    rollout,
    table,
    mixed,
    scores,
    head,
    out0,
    in0,
    total_a,
    total_b,
    *rest,
):
    bufs_a, bufs_b = rest[:6], rest[6:12]
    head_a, head_b, buf_a, buf_b = rest[12:16]
    load_sem, pair_send, pair_recv, sum_send, sum_recv = rest[16:21]
    head_send, head_recv, all_send, all_recv = rest[21:]
    here = Place()
    met = greet(here)

    loads = [pltpu.make_async_copy(table_hbm, table, load_sem.at[0])]
    tiles = [pl.ds(TILE * i, TILE) for i in range(4)]
    for i, rows in enumerate(tiles):
        loads.append(
            pltpu.make_async_copy(hidden_hbm.at[rows], features.at[rows], load_sem.at[1 + i])
        )
    loads.append(pltpu.make_async_copy(roll_hbm, rollout, load_sem.at[5]))
    small = [
        (shard_hbm, shard),
        (tokens_hbm, ints.at[0:8]),
        (action_hbm, ints.at[8:16]),
        (roll_tokens_hbm, roll_ints.at[0]),
        (roll_action_hbm, roll_ints.at[1]),
        (returns_hbm, returns),
        (episode_hbm, episode),
        (gain_hbm, gain),
    ]
    small = [
        pltpu.make_async_copy(src, dst, load_sem.at[6 + i]) for i, (src, dst) in enumerate(small)
    ]
    for load in small:
        load.start()
    loads[0].start()
    loads[1].start()

    small[0].wait()
    rows = pl.ds(pl.multiple_of(here.y_hi * ROWS, ROWS), ROWS)
    for part, (buf, spot) in enumerate(((head_a, (here.y, here.x)), (head_b, (here.x, here.y)))):
        cols = pl.ds(pl.multiple_of(here.core * HALF + part * PART, PART), PART)
        buf[here.core, spot[0], spot[1], here.z] = shard[rows, cols]
    met()
    walk = gather_walk(head_a, head_b, here, (head_send, head_recv))
    next(walk)
    turn = itertools.count(1)

    def step():
        if next(turn) in (6, 9, 10, 11, 12, 13, 14, 15, 16, 17, 18, 19, 20, 21, 22, 23):
            next(walk, None)

    for load in small[1:]:
        load.wait()
    numbers = columns_of(ints[...].astype(jnp.float32))
    beside = jnp.concatenate([roll_ints[0], roll_ints[1]], axis=1).astype(jnp.float32)
    roll_numbers = columns_of(jnp.broadcast_to(beside, (8, 128)))
    advantage = columns_of(advantage_of(returns[...], episode[...]))

    def column(values, first, tile):
        return jnp.concatenate([values[:, first + 2 * tile + j][:, None] for j in range(2)], axis=0)

    loads[0].wait()
    for i, rows in enumerate(tiles):
        loads[2 + i].start()
        loads[1 + i].wait()
        station_rows(features.at[rows], column(numbers, 0, i), table, gain, mixed, step)
    loads[5].wait()
    station_rows(rollout, roll_numbers[:STEPS, :1], table, gain, mixed, step)
    for _ in walk:
        pass
    for core, y, x in itertools.product(range(2), range(NY), range(NX)):
        for part, blocks in enumerate((head_a[core, y, x], head_b[core, x, y])):
            head[y % 2, x, :, y // 2, :, pl.ds(core * HALF + part * PART, PART)] = blocks

    for i, rows in enumerate(tiles):
        logits = jnp.dot(
            features[rows, :],
            head[...].reshape(D, ACTIONS),
            preferred_element_type=jnp.float32,
        )
        expo = jnp.exp(logits - jnp.max(logits, axis=-1, keepdims=True))
        probs = expo / jnp.sum(expo, axis=-1, keepdims=True)
        chosen = one_hot(column(numbers, 8, i), ACTIONS).astype(jnp.float32)
        value = (column(advantage, 0, i) * (probs - chosen)).astype(jnp.bfloat16)
        scores[0, rows] = value[:, :HALF]
        scores[1, rows] = value[:, HALF:]

    sems = (sum_send, sum_recv)
    first_a, direct_a, rest_a = sum_part(
        total_a, here.y, here.x, here.along_y, here.along_x, bufs_a, here, sems, 0
    )
    first_b, direct_b, rest_b = sum_part(
        total_b, here.x, here.y, here.along_x, here.along_y, bufs_b, here, sems, SUM_SEMS
    )
    pairs = []
    mine, theirs = scores[here.core], scores[1 - here.core]

    def chunk(far, dx):
        y_lo = lax.rem(here.y + far, 2)
        return y_lo, lax.rem(here.x + dx, NX)

    def make(far, dx):
        y_lo, x = chunk(far, dx)
        cols = pl.ds(pl.multiple_of(y_lo * (D // 2) + x * 512, 512), 512)
        left = jnp.transpose(features[:, cols])
        k = len(pairs)
        out0[k] = jnp.dot(left, theirs, preferred_element_type=jnp.float32).astype(jnp.bfloat16)
        pairs.append(send(out0.at[k], in0.at[k], (pair_send, pair_recv), k, here.sibling()))
        own = jnp.dot(left, mine, preferred_element_type=jnp.float32).reshape(NZ, 2, ROWS, HALF)
        for y_hi in range(2):
            total_a[2 * y_hi + y_lo, x] = own[:, y_hi, :, :PART]
            total_b[x, 2 * y_hi + y_lo] = own[:, y_hi, :, PART:]

    def both(k, far, dx):
        y_lo, x = chunk(far, dx)
        pairs[k].wait_recv()
        other = in0[k].astype(jnp.float32).reshape(NZ, 2, ROWS, HALF)
        for y_hi in range(2):
            y = 2 * y_hi + y_lo
            total_a[y, x] = total_a[y, x] + other[:, y_hi, :, :PART]
            total_b[x, y] = total_b[x, y] + other[:, y_hi, :, PART:]

    ready = [
        ((0, 2), [(first_b, 2), (first_a, 2), (first_b, 0)]),
        ((1, 2), [(first_b, 1), (first_b, 3), (direct_a, 2)]),
        ((0, 1), [(first_a, 1)]),
        ((0, 3), [(first_a, 3), (direct_b, 2), (direct_b, 0)]),
        ((0, 0), [(first_a, 0)]),
        ((1, 1), [(direct_a, 1), (direct_b, 1), (direct_b, 3)]),
        ((1, 3), [(direct_a, 3)]),
        ((1, 0), [(direct_a, 0)]),
    ]

    def settle(k):
        both(k, *ready[k][0])
        for post, distance in ready[k][1]:
            post(distance)

    summing = itertools.zip_longest(rest_a(), rest_b())
    next(summing)
    for k, (where, _) in enumerate(ready):
        make(*where)
        if k:
            settle(k - 1)
        if k >= 6:
            next(summing)
    settle(7)
    for copy in pairs:
        copy.wait_send()

    for _ in summing:
        pass

    buf_a[here.core, here.y, here.x, here.z] = total_a[here.y, here.x, here.z].astype(jnp.bfloat16)
    buf_b[here.core, here.x, here.y, here.z] = total_b[here.x, here.y, here.z].astype(jnp.bfloat16)
    for _ in gather_walk(buf_a, buf_b, here, (all_send, all_recv)):
        pass

    squares = jnp.zeros((ROWS, PART), jnp.float32)
    for core, y, x in itertools.product(range(2), range(NY), range(NX)):
        for block in (buf_a[core, y, x], buf_b[core, x, y]):
            block = block.astype(jnp.float32)
            squares = squares + jnp.sum(block * block, axis=0)
    scale = step_length * lax.rsqrt(jnp.sum(squares, keepdims=True) + 1e-06)
    for core, y, x in itertools.product(range(2), range(NY), range(NX)):
        for part, block in enumerate((buf_a[core, y, x], buf_b[core, x, y])):
            cols = pl.ds(core * HALF + part * PART, PART)
            old = head[y % 2, x, :, y // 2, :, cols].astype(jnp.float32)
            change = block.astype(jnp.float32) * scale.reshape(1, 1, 1)
            head[y % 2, x, :, y // 2, :, cols] = (old - change).astype(jnp.bfloat16)
    new_ref[...] = head[lax.rem(here.y, 2), here.x, here.z].reshape(2 * ROWS, ACTIONS)
    new_store = pltpu.make_async_copy(new_ref, new_hbm, load_sem.at[2])
    new_store.start()
    logits = jnp.dot(
        rollout[...], head[...].reshape(D, ACTIONS), preferred_element_type=jnp.float32
    )
    top = jnp.max(logits, axis=-1, keepdims=True)
    total = jnp.log(jnp.sum(jnp.exp(logits - top), axis=-1, keepdims=True)) + top
    chosen = one_hot(roll_numbers[STEPS:, :1], ACTIONS).astype(jnp.float32)
    logp = jnp.sum(logits * chosen, axis=-1, keepdims=True) - total
    logp_ref[...] = jnp.transpose(jnp.broadcast_to(logp, (STEPS, 128)))[:1, :]
    episode_ref[...] = jnp.broadcast_to(jnp.sum(logp, keepdims=True), (1, 128))
    stores = [
        pltpu.make_async_copy(src, dst, load_sem.at[i])
        for i, (src, dst) in enumerate(((logp_ref, logp_hbm), (episode_ref, episode_logp_hbm)))
    ]
    for store in stores:
        store.start()
    for store in stores + [new_store]:
        store.wait()


SPREAD = (2, NX, NZ, 2, ROWS, ACTIONS)


def dma_sems(count):
    return [pltpu.SemaphoreType.DMA((count,)), pltpu.SemaphoreType.DMA((count,))]


def gather_buffers():
    return [
        pltpu.VMEM((2, NY, NX, NZ, ROWS, PART), jnp.bfloat16),
        pltpu.VMEM((2, NX, NY, NZ, ROWS, PART), jnp.bfloat16),
    ]


def hand_over(*refs):
    for source, target in zip(refs[:3], refs[3:]):
        target[...] = source[...]


def results(*arrays):
    vmem = pl.BlockSpec(memory_space=pltpu.VMEM)
    return pl.pallas_call(
        hand_over,
        out_shape=tuple(jax.ShapeDtypeStruct(a.shape, a.dtype) for a in arrays),
        in_specs=[vmem] * 3,
        out_specs=(vmem,) * 3,
    )(*arrays)


def whole_step(*arrays):
    anywhere = pl.BlockSpec(memory_space=pl.ANY)
    return pl.pallas_call(
        whole_kernel,
        out_shape=(
            jax.ShapeDtypeStruct((2 * ROWS, ACTIONS), jnp.bfloat16),
            jax.ShapeDtypeStruct((1, STEPS), jnp.float32),
            jax.ShapeDtypeStruct((1, 128), jnp.float32),
        ),
        in_specs=[anywhere] * len(arrays),
        out_specs=(anywhere,) * 3,
        scratch_shapes=[
            pltpu.VMEM((1, D), jnp.float32),
            pltpu.VMEM((16, 128), jnp.int32),
            pltpu.VMEM((2, 1, STEPS), jnp.int32),
            pltpu.VMEM((8, 128), jnp.float32),
            pltpu.VMEM((8, 128), jnp.int32),
            pltpu.VMEM((2 * ROWS, ACTIONS), jnp.bfloat16),
            pltpu.VMEM((2 * ROWS, ACTIONS), jnp.bfloat16),
            pltpu.VMEM((1, STEPS), jnp.float32),
            pltpu.VMEM((1, 128), jnp.float32),
            pltpu.VMEM((1024, D), jnp.bfloat16),
            pltpu.VMEM((STEPS, D), jnp.bfloat16),
            pltpu.VMEM((STATIONS, D), jnp.bfloat16),
            pltpu.VMEM((TILE, D), jnp.float32),
            pltpu.VMEM((2, 1024, HALF), jnp.bfloat16),
            pltpu.VMEM(SPREAD, jnp.bfloat16),
            pltpu.VMEM((8, 512, HALF), jnp.bfloat16),
            pltpu.VMEM((8, 512, HALF), jnp.bfloat16),
            pltpu.VMEM((NY, NX, NZ, ROWS, PART), jnp.float32),
            pltpu.VMEM((NX, NY, NZ, ROWS, PART), jnp.float32),
            *part_buffers(),
            *part_buffers(),
            *gather_buffers(),
            *gather_buffers(),
            pltpu.SemaphoreType.DMA((14,)),
            *dma_sems(8),
            *dma_sems(2 * SUM_SEMS),
            *dma_sems(2 * GATHER_SEMS),
            *dma_sems(2 * GATHER_SEMS),
        ],
        compiler_params=pltpu.CompilerParams(
            collective_id=0, has_side_effects=True, vmem_limit_bytes=60 << 20
        ),
    )(*arrays)


def local(
    traj_hidden,
    traj_tokens,
    traj_action,
    traj_return,
    traj_episode,
    roll_hidden,
    roll_tokens,
    roll_action,
    station_table,
    norm_gain,
    head_weight,
):
    arrays = whole_step(
        traj_hidden,
        roll_hidden,
        station_table,
        norm_gain.reshape(1, D),
        traj_tokens.reshape(8, 128),
        traj_action.reshape(8, 128),
        roll_tokens.reshape(1, STEPS),
        roll_action.reshape(1, STEPS),
        traj_return.reshape(8, 128),
        traj_episode.reshape(8, 128),
        head_weight,
    )
    new_head, action_logp, episode_logp = results(*arrays)
    return (new_head, action_logp.reshape(STEPS), episode_logp[0, :1])


def solution(mesh):
    placed = (
        P(("grp", "fsdp"), None),
        P(("grp", "fsdp")),
        P(("grp", "fsdp")),
        P(("grp", "fsdp")),
        P(("grp", "fsdp"), None),
        P(("grp", "fsdp"), None),
        P(("grp", "fsdp")),
        P(("grp", "fsdp")),
        P(),
        P(),
        P("fsdp", None),
    )
    return jax.shard_map(
        local,
        mesh=mesh,
        in_specs=placed,
        out_specs=(P("fsdp", None), P(("grp", "fsdp")), P(("grp", "fsdp"))),
        check_vma=False,
    )
```

```python
import itertools

import jax
import jax.numpy as jnp
from jax import lax
from jax.experimental import pallas as pl
from jax.experimental.pallas import tpu as pltpu
from jax.sharding import PartitionSpec as P

ACTIONS = 512
STATIONS = 512
EPI_BLK = 8
STEPS = 64
D = 4096
MESH = pl.DeviceIdType.MESH
NY, NX, NZ = 4, 4, 8
ROWS = 32
HALF = 256
PART = 128

step_length = 8.0


class Place:
    def __init__(self):
        grp, shard = lax.axis_index("grp"), lax.axis_index("fsdp")
        self.core = lax.rem(grp, 2)
        self.y = lax.div(grp, 2) * 2 + lax.div(shard, 32)
        self.x = lax.rem(lax.div(shard, 8), 4)
        self.z = lax.rem(shard, 8)
        self.y_hi = lax.div(grp, 2)
        self.shard = shard

    def at(self, y=None, x=None, z=None, core=None):
        y = self.y if y is None else y
        x = self.x if x is None else x
        z = self.z if z is None else z
        core = self.core if core is None else core
        return (lax.div(y, 2) * 2 + core, lax.rem(y, 2) * 32 + x * 8 + z)

    def sibling(self):
        return self.at(core=1 - self.core)

    def along_z(self, k):
        return self.at(z=lax.rem(self.z + k, NZ))

    def along_y(self, k):
        return self.at(y=lax.rem(self.y + k, NY))

    def along_x(self, k):
        return self.at(x=lax.rem(self.x + k, NX))


def greet(here):
    barrier = pltpu.get_barrier_semaphore()
    friends = [here.along_z(k) for k in range(1, NZ)]
    friends += [here.along_y(k) for k in range(1, NY)] + [here.along_x(k) for k in range(1, NX)]
    friends += [here.sibling()]
    for friend in friends:
        pl.semaphore_signal(barrier, inc=1, device_id=friend, device_id_type=MESH)
    return lambda: pl.semaphore_wait(barrier, len(friends))


def send(src, dst, sems, index, device):
    copy = pltpu.make_async_remote_copy(
        src_ref=src,
        dst_ref=dst,
        send_sem=sems[0].at[index],
        recv_sem=sems[1].at[index],
        device_id=device,
        device_id_type=MESH,
    )
    copy.start()
    return copy


def together(*walks):
    for _ in itertools.zip_longest(*walks):
        pass


GATHER_SEMS = 7 + 3 + 12 + 16


def gather_part(buf, outer, inner, along_outer, along_inner, here, sems, base, landed=None):
    core, z = here.core, here.z
    numbers = itertools.count(base)
    sends, shared, waiting = [], [], []
    plus, minus = along_outer(1), along_outer(3)

    def put(block, device):
        copy = send(block, block, sems, next(numbers), device)
        sends.append(copy)
        return copy

    def report(which, dy, dx):
        if landed is not None:
            landed(which, lax.rem(outer + dy, 4), lax.rem(inner + dx, 4))

    def receive():
        dy, dx, copy = waiting.pop(0)
        copy.wait_recv()
        report(1 - core, dy, dx)

    def share(dy, dx):
        block = spot(dy, dx)
        copy = send(block, block, sems, next(numbers), here.sibling())
        shared.append(copy)
        waiting.append((dy, dx, copy))
        report(core, dy, dx)
        if landed is not None and len(waiting) > 4:
            receive()

    def spot(dy, dx):
        return buf.at[core, lax.rem(outer + dy, 4), lax.rem(inner + dx, 4)]

    mine = buf.at[core, outer, inner, z]
    along_z = [put(mine, here.along_z(k)) for k in (1, 7, 2, 6, 3, 5, 4)]
    yield
    for copy in along_z:
        copy.wait_recv()
    inside = {4 - k: put(spot(0, 0), along_inner(k)) for k in (1, 3, 2)}
    up, down = {0: put(spot(0, 0), plus)}, {0: put(spot(0, 0), minus)}
    share(0, 0)
    onward = []

    def spread(k):
        inside[k].wait_recv()
        up[k], down[k] = put(spot(0, k), plus), put(spot(0, k), minus)
        if k == 2:
            onward.append((k, put(spot(0, k), along_outer(2))))
        share(0, k)

    def from_below(k):
        up[k].wait_recv()
        if k in (0, 3):
            onward.append((k, put(spot(3, k), plus)))
        share(3, k)

    def from_above(k):
        down[k].wait_recv()
        if k == 1:
            onward.append((k, put(spot(1, k), minus)))
        share(1, k)

    yield
    spread(1)
    yield
    spread(3)
    yield
    from_below(0)
    yield
    spread(2)
    for k in (1, 3, 2):
        yield
        from_above(k)
        yield
        from_below(k)
    yield
    from_above(0)
    for k, copy in sorted(onward, key=lambda one: one[0] == 2):
        yield
        copy.wait_recv()
        share(2, k)
    yield
    while waiting:
        receive()
    for copy in sends + shared:
        copy.wait_send()


def gather_walk(buf_a, buf_b, here, sems, landed_a=None, landed_b=None):
    y, x = (here.y, here.along_y), (here.x, here.along_x)
    return itertools.zip_longest(
        gather_part(buf_a, y[0], x[0], y[1], x[1], here, sems, 0, landed_a),
        gather_part(buf_b, x[0], y[0], x[1], y[1], here, sems, GATHER_SEMS, landed_b),
    )


SUM_SEMS = 12 + 3 + 7


def sum_part(total, outer, inner, along_outer, along_inner, bufs, here, sems, base):
    out1, in1, out2, in2, out3, in3 = bufs
    plus, minus = along_outer(1), along_outer(3)
    sends = []

    def block(dy, dx):
        return total.at[lax.rem(outer + dy, 4), lax.rem(inner + dx, 4)]

    def post(out, come, slot, value, device, number):
        out[slot] = value.astype(jnp.bfloat16)
        copy = send(out.at[slot], come.at[slot], sems, base + number, device)
        sends.append(copy)
        return copy

    def ring(slot, value, device):
        return post(out1, in1, slot, value, device, slot)

    def got(come, slot):
        return come[slot].astype(jnp.float32)

    order = (2, 1, 3, 0)
    spots = {k: i for i, k in enumerate(order)}
    up, down = (plus, minus, 1, 3), (minus, plus, 3, 1)
    way = {2: up, 0: up, 1: down, 3: down}
    first, direct, last = {}, {}, {}

    def post_first(k):
        first[k] = ring(spots[k], block(2, k)[...], way[k][0])

    def post_direct(k):
        direct[k] = ring(4 + spots[k], block(way[k][3], k)[...], way[k][1])

    inside = {}

    def finish(i, k):
        last[k].wait_recv()
        direct[k].wait_recv()
        value = block(0, k)[...] + got(in1, 4 + i) + got(in1, 8 + i)
        if k == 0:
            block(0, 0)[...] = value
        else:
            inside[k] = post(out2, in2, k - 1, value, along_inner(k), 11 + k)

    def rest():
        for i, k in enumerate(order):
            yield
            first[k].wait_recv()
            last[k] = ring(8 + i, block(way[k][2], k)[...] + got(in1, i), way[k][0])
        for i, k in enumerate(order):
            yield
            finish(i, k)
        for k in (1, 3, 2):
            yield
            inside[k].wait_recv()
            block(0, 0)[...] = block(0, 0)[...] + got(in2, k - 1)
        along_z = []
        for k in (1, 7, 2, 6, 3, 5, 4):
            value = total[outer, inner, lax.rem(here.z + k, NZ)]
            along_z.append((k, post(out3, in3, k - 1, value, here.along_z(k), 14 + k)))
        yield
        value = total[outer, inner, here.z]
        for k, copy in along_z:
            copy.wait_recv()
            value = value + got(in3, k - 1)
        total[outer, inner, here.z] = value
        for copy in sends:
            copy.wait_send()

    return post_first, post_direct, rest


def part_buffers():
    bf = jnp.bfloat16
    return [
        pltpu.VMEM((12, NZ, ROWS, PART), bf),
        pltpu.VMEM((12, NZ, ROWS, PART), bf),
        pltpu.VMEM((3, NZ, ROWS, PART), bf),
        pltpu.VMEM((3, NZ, ROWS, PART), bf),
        pltpu.VMEM((NZ - 1, ROWS, PART), bf),
        pltpu.VMEM((NZ - 1, ROWS, PART), bf),
    ]


TILE = 256
WIDE = 1024


def one_hot(column, count):
    spots = lax.broadcasted_iota(jnp.int32, (column.shape[0], count), 1).astype(jnp.float32)
    return column == spots


def columns_of(rows):
    return jnp.transpose(rows)


def advantage_of(returns, episode):
    baseline = jnp.zeros_like(returns)
    for number in range(EPI_BLK):
        member = (episode == number).astype(jnp.float32)
        total = jnp.sum(returns * member, keepdims=True)
        count = jnp.sum(member, keepdims=True)
        baseline = baseline + member * (total / count)
    return returns - baseline


def station_rows(rows_ref, tokens, table, gain, mixed, step):
    n = rows_ref.shape[0]
    lookup = one_hot(tokens, STATIONS).astype(jnp.bfloat16)
    power = jnp.zeros((n, 1), jnp.float32)
    for left in range(0, D, WIDE):
        cols = pl.ds(left, WIDE)
        value = rows_ref[:, cols].astype(jnp.float32) + jnp.dot(
            lookup, table[:, cols], preferred_element_type=jnp.float32
        )
        mixed[:n, cols] = value
        power = power + jnp.sum(value * value, axis=-1, keepdims=True)
        step()
    inverse = lax.rsqrt(power * (1.0 / D) + 1e-05)
    for left in range(0, D, WIDE):
        cols = pl.ds(left, WIDE)
        rows_ref[:, cols] = (mixed[:n, cols] * inverse * gain[:, cols]).astype(jnp.bfloat16)
    step()


def whole_kernel(
    hidden_hbm,
    roll_hbm,
    table_hbm,
    gain_hbm,
    tokens_hbm,
    action_hbm,
    roll_tokens_hbm,
    roll_action_hbm,
    returns_hbm,
    episode_hbm,
    shard_hbm,
    new_hbm,
    logp_hbm,
    episode_logp_hbm,
    gain,
    ints,
    roll_ints,
    returns,
    episode,
    shard,
    new_ref,
    logp_ref,
    episode_ref,
    features,
    rollout,
    table,
    mixed,
    scores,
    head,
    squares,
    out0,
    in0,
    total_a,
    total_b,
    *rest,
):
    bufs_a, bufs_b = rest[:6], rest[6:12]
    head_a, head_b, buf_a, buf_b = rest[12:16]
    load_sem, pair_send, pair_recv, sum_send, sum_recv = rest[16:21]
    head_send, head_recv, all_send, all_recv = rest[21:]
    here = Place()
    met = greet(here)

    loads = [pltpu.make_async_copy(table_hbm, table, load_sem.at[0])]
    tiles = [pl.ds(TILE * i, TILE) for i in range(4)]
    for i, rows in enumerate(tiles):
        loads.append(
            pltpu.make_async_copy(hidden_hbm.at[rows], features.at[rows], load_sem.at[1 + i])
        )
    loads.append(pltpu.make_async_copy(roll_hbm, rollout, load_sem.at[5]))
    small = [
        (shard_hbm, shard),
        (tokens_hbm, ints.at[0:8]),
        (action_hbm, ints.at[8:16]),
        (roll_tokens_hbm, roll_ints.at[0]),
        (roll_action_hbm, roll_ints.at[1]),
        (returns_hbm, returns),
        (episode_hbm, episode),
        (gain_hbm, gain),
    ]
    small = [
        pltpu.make_async_copy(src, dst, load_sem.at[6 + i]) for i, (src, dst) in enumerate(small)
    ]
    for load in small:
        load.start()
    loads[0].start()
    loads[1].start()

    small[0].wait()
    rows = pl.ds(pl.multiple_of(here.y_hi * ROWS, ROWS), ROWS)
    for part, (buf, spot) in enumerate(((head_a, (here.y, here.x)), (head_b, (here.x, here.y)))):
        cols = pl.ds(pl.multiple_of(here.core * HALF + part * PART, PART), PART)
        buf[here.core, spot[0], spot[1], here.z] = shard[rows, cols]
    met()
    walk = gather_walk(head_a, head_b, here, (head_send, head_recv))
    next(walk)
    turn = itertools.count(1)

    def step():
        if next(turn) in (6, 9, 10, 11, 12, 13, 14, 15, 16, 17, 18, 19, 20, 21, 22, 23):
            next(walk, None)

    for load in small[1:]:
        load.wait()
    numbers = columns_of(ints[...].astype(jnp.float32))
    beside = jnp.concatenate([roll_ints[0], roll_ints[1]], axis=1).astype(jnp.float32)
    roll_numbers = columns_of(jnp.broadcast_to(beside, (8, 128)))
    advantage = columns_of(advantage_of(returns[...], episode[...]))

    def column(values, first, tile):
        return jnp.concatenate([values[:, first + 2 * tile + j][:, None] for j in range(2)], axis=0)

    loads[0].wait()
    for i, rows in enumerate(tiles):
        loads[2 + i].start()
        loads[1 + i].wait()
        station_rows(features.at[rows], column(numbers, 0, i), table, gain, mixed, step)
    loads[5].wait()
    station_rows(rollout, roll_numbers[:STEPS, :1], table, gain, mixed, step)
    for _ in walk:
        pass
    for core, y, x in itertools.product(range(2), range(NY), range(NX)):
        for part, blocks in enumerate((head_a[core, y, x], head_b[core, x, y])):
            head[y % 2, x, :, y // 2, :, pl.ds(core * HALF + part * PART, PART)] = blocks

    for i, rows in enumerate(tiles):
        logits = jnp.dot(
            features[rows, :],
            head[...].reshape(D, ACTIONS),
            preferred_element_type=jnp.float32,
        )
        expo = jnp.exp(logits - jnp.max(logits, axis=-1, keepdims=True))
        probs = expo / jnp.sum(expo, axis=-1, keepdims=True)
        chosen = one_hot(column(numbers, 8, i), ACTIONS).astype(jnp.float32)
        value = (column(advantage, 0, i) * (probs - chosen)).astype(jnp.bfloat16)
        scores[0, rows] = value[:, :HALF]
        scores[1, rows] = value[:, HALF:]

    sems = (sum_send, sum_recv)
    first_a, direct_a, rest_a = sum_part(
        total_a, here.y, here.x, here.along_y, here.along_x, bufs_a, here, sems, 0
    )
    first_b, direct_b, rest_b = sum_part(
        total_b, here.x, here.y, here.along_x, here.along_y, bufs_b, here, sems, SUM_SEMS
    )
    pairs = []
    mine, theirs = scores[here.core], scores[1 - here.core]

    def chunk(far, dx):
        y_lo = lax.rem(here.y + far, 2)
        return y_lo, lax.rem(here.x + dx, NX)

    def make(far, dx):
        y_lo, x = chunk(far, dx)
        cols = pl.ds(pl.multiple_of(y_lo * (D // 2) + x * 512, 512), 512)
        left = jnp.transpose(features[:, cols])
        k = len(pairs)
        out0[k] = jnp.dot(left, theirs, preferred_element_type=jnp.float32).astype(jnp.bfloat16)
        pairs.append(send(out0.at[k], in0.at[k], (pair_send, pair_recv), k, here.sibling()))
        own = jnp.dot(left, mine, preferred_element_type=jnp.float32).reshape(NZ, 2, ROWS, HALF)
        for y_hi in range(2):
            total_a[2 * y_hi + y_lo, x] = own[:, y_hi, :, :PART]
            total_b[x, 2 * y_hi + y_lo] = own[:, y_hi, :, PART:]

    def both(k, far, dx):
        y_lo, x = chunk(far, dx)
        pairs[k].wait_recv()
        other = in0[k].astype(jnp.float32).reshape(NZ, 2, ROWS, HALF)
        for y_hi in range(2):
            y = 2 * y_hi + y_lo
            total_a[y, x] = total_a[y, x] + other[:, y_hi, :, :PART]
            total_b[x, y] = total_b[x, y] + other[:, y_hi, :, PART:]

    ready = [
        ((0, 2), [(first_b, 2), (first_a, 2), (first_b, 0)]),
        ((1, 2), [(first_b, 1), (first_b, 3), (direct_a, 2)]),
        ((0, 1), [(first_a, 1)]),
        ((0, 3), [(first_a, 3), (direct_b, 2), (direct_b, 0)]),
        ((0, 0), [(first_a, 0)]),
        ((1, 1), [(direct_a, 1), (direct_b, 1), (direct_b, 3)]),
        ((1, 3), [(direct_a, 3)]),
        ((1, 0), [(direct_a, 0)]),
    ]

    def settle(k):
        both(k, *ready[k][0])
        for post, distance in ready[k][1]:
            post(distance)

    summing = itertools.zip_longest(rest_a(), rest_b())
    next(summing)
    for k, (where, _) in enumerate(ready):
        make(*where)
        if k:
            settle(k - 1)
        if k >= 6:
            next(summing)
    settle(7)
    for copy in pairs:
        copy.wait_send()

    for turn, _ in enumerate(summing):
        if turn == 8:
            mixed[:STEPS, :ACTIONS] = jnp.dot(
                rollout[...], head[...].reshape(D, ACTIONS), preferred_element_type=jnp.float32
            )
            shard[...] = head[lax.rem(here.y, 2), here.x, here.z].reshape(2 * ROWS, ACTIONS)

    buf_a[here.core, here.y, here.x, here.z] = total_a[here.y, here.x, here.z].astype(jnp.bfloat16)
    buf_b[here.core, here.x, here.y, here.z] = total_b[here.x, here.y, here.z].astype(jnp.bfloat16)

    def landing(part, buf, y_first):
        def landed(core, a, b):
            y, x = (a, b) if y_first else (b, a)
            block = buf[core, a, b]
            cols = pl.ds(pl.multiple_of(core * HALF + part * PART, PART), PART)
            head[lax.rem(y, 2), x, :, lax.div(y, 2), :, cols] = block
            block = block.astype(jnp.float32)
            squares[core, part, y, x] = jnp.sum((block * block).reshape(-1, 8, PART), axis=0)

        return landed

    for _ in gather_walk(
        buf_a,
        buf_b,
        here,
        (all_send, all_recv),
        landing(0, buf_a, True),
        landing(1, buf_b, False),
    ):
        pass

    scale = step_length * lax.rsqrt(jnp.sum(squares[...], keepdims=True).reshape(1, 1) + 1e-06)
    change = head[lax.rem(here.y, 2), here.x, here.z].reshape(2 * ROWS, ACTIONS)
    new_ref[...] = (
        shard[...].astype(jnp.float32) - change.astype(jnp.float32) * scale
    ).astype(jnp.bfloat16)
    new_store = pltpu.make_async_copy(new_ref, new_hbm, load_sem.at[2])
    new_store.start()
    logits = mixed[:STEPS, :ACTIONS] - scale * jnp.dot(
        rollout[...], head[...].reshape(D, ACTIONS), preferred_element_type=jnp.float32
    )
    top = jnp.max(logits, axis=-1, keepdims=True)
    total = jnp.log(jnp.sum(jnp.exp(logits - top), axis=-1, keepdims=True)) + top
    chosen = one_hot(roll_numbers[STEPS:, :1], ACTIONS).astype(jnp.float32)
    logp = jnp.sum(logits * chosen, axis=-1, keepdims=True) - total
    logp_ref[...] = jnp.transpose(jnp.broadcast_to(logp, (STEPS, 128)))[:1, :]
    episode_ref[...] = jnp.broadcast_to(jnp.sum(logp, keepdims=True), (1, 128))
    stores = [
        pltpu.make_async_copy(src, dst, load_sem.at[i])
        for i, (src, dst) in enumerate(((logp_ref, logp_hbm), (episode_ref, episode_logp_hbm)))
    ]
    for store in stores:
        store.start()
    for store in stores + [new_store]:
        store.wait()


SPREAD = (2, NX, NZ, 2, ROWS, ACTIONS)


def dma_sems(count):
    return [pltpu.SemaphoreType.DMA((count,)), pltpu.SemaphoreType.DMA((count,))]


def gather_buffers():
    return [
        pltpu.VMEM((2, NY, NX, NZ, ROWS, PART), jnp.bfloat16),
        pltpu.VMEM((2, NX, NY, NZ, ROWS, PART), jnp.bfloat16),
    ]


def hand_over(*refs):
    for source, target in zip(refs[:3], refs[3:]):
        target[...] = source[...]


def results(*arrays):
    vmem = pl.BlockSpec(memory_space=pltpu.VMEM)
    return pl.pallas_call(
        hand_over,
        out_shape=tuple(jax.ShapeDtypeStruct(a.shape, a.dtype) for a in arrays),
        in_specs=[vmem] * 3,
        out_specs=(vmem,) * 3,
    )(*arrays)


def whole_step(*arrays):
    anywhere = pl.BlockSpec(memory_space=pl.ANY)
    return pl.pallas_call(
        whole_kernel,
        out_shape=(
            jax.ShapeDtypeStruct((2 * ROWS, ACTIONS), jnp.bfloat16),
            jax.ShapeDtypeStruct((1, STEPS), jnp.float32),
            jax.ShapeDtypeStruct((1, 128), jnp.float32),
        ),
        in_specs=[anywhere] * len(arrays),
        out_specs=(anywhere,) * 3,
        scratch_shapes=[
            pltpu.VMEM((1, D), jnp.float32),
            pltpu.VMEM((16, 128), jnp.int32),
            pltpu.VMEM((2, 1, STEPS), jnp.int32),
            pltpu.VMEM((8, 128), jnp.float32),
            pltpu.VMEM((8, 128), jnp.int32),
            pltpu.VMEM((2 * ROWS, ACTIONS), jnp.bfloat16),
            pltpu.VMEM((2 * ROWS, ACTIONS), jnp.bfloat16),
            pltpu.VMEM((1, STEPS), jnp.float32),
            pltpu.VMEM((1, 128), jnp.float32),
            pltpu.VMEM((1024, D), jnp.bfloat16),
            pltpu.VMEM((STEPS, D), jnp.bfloat16),
            pltpu.VMEM((STATIONS, D), jnp.bfloat16),
            pltpu.VMEM((TILE, D), jnp.float32),
            pltpu.VMEM((2, 1024, HALF), jnp.bfloat16),
            pltpu.VMEM(SPREAD, jnp.bfloat16),
            pltpu.VMEM((2, 2, NY, NX, 8, PART), jnp.float32),
            pltpu.VMEM((8, 512, HALF), jnp.bfloat16),
            pltpu.VMEM((8, 512, HALF), jnp.bfloat16),
            pltpu.VMEM((NY, NX, NZ, ROWS, PART), jnp.float32),
            pltpu.VMEM((NX, NY, NZ, ROWS, PART), jnp.float32),
            *part_buffers(),
            *part_buffers(),
            *gather_buffers(),
            *gather_buffers(),
            pltpu.SemaphoreType.DMA((14,)),
            *dma_sems(8),
            *dma_sems(2 * SUM_SEMS),
            *dma_sems(2 * GATHER_SEMS),
            *dma_sems(2 * GATHER_SEMS),
        ],
        compiler_params=pltpu.CompilerParams(
            collective_id=0, has_side_effects=True, vmem_limit_bytes=60 << 20
        ),
    )(*arrays)


def local(
    traj_hidden,
    traj_tokens,
    traj_action,
    traj_return,
    traj_episode,
    roll_hidden,
    roll_tokens,
    roll_action,
    station_table,
    norm_gain,
    head_weight,
):
    arrays = whole_step(
        traj_hidden,
        roll_hidden,
        station_table,
        norm_gain.reshape(1, D),
        traj_tokens.reshape(8, 128),
        traj_action.reshape(8, 128),
        roll_tokens.reshape(1, STEPS),
        roll_action.reshape(1, STEPS),
        traj_return.reshape(8, 128),
        traj_episode.reshape(8, 128),
        head_weight,
    )
    new_head, action_logp, episode_logp = results(*arrays)
    return (new_head, action_logp.reshape(STEPS), episode_logp[0, :1])


def solution(mesh):
    placed = (
        P(("grp", "fsdp"), None),
        P(("grp", "fsdp")),
        P(("grp", "fsdp")),
        P(("grp", "fsdp")),
        P(("grp", "fsdp"), None),
        P(("grp", "fsdp"), None),
        P(("grp", "fsdp")),
        P(("grp", "fsdp")),
        P(),
        P(),
        P("fsdp", None),
    )
    return jax.shard_map(
        local,
        mesh=mesh,
        in_specs=placed,
        out_specs=(P("fsdp", None), P(("grp", "fsdp")), P(("grp", "fsdp"))),
        check_vma=False,
    )
```

```python
import itertools

import jax
import jax.numpy as jnp
from jax import lax
from jax.experimental import pallas as pl
from jax.experimental.pallas import tpu as pltpu
from jax.sharding import PartitionSpec as P

ACTIONS = 512
STATIONS = 512
EPI_BLK = 8
STEPS = 64
D = 4096
MESH = pl.DeviceIdType.MESH
NY, NX, NZ = 4, 4, 8
ROWS = 32
HALF = 256
PART = 128

step_length = 8.0


class Place:
    def __init__(self):
        grp, shard = lax.axis_index("grp"), lax.axis_index("fsdp")
        self.core = lax.rem(grp, 2)
        self.y = lax.div(grp, 2) * 2 + lax.div(shard, 32)
        self.x = lax.rem(lax.div(shard, 8), 4)
        self.z = lax.rem(shard, 8)
        self.y_hi = lax.div(grp, 2)
        self.shard = shard

    def at(self, y=None, x=None, z=None, core=None):
        y = self.y if y is None else y
        x = self.x if x is None else x
        z = self.z if z is None else z
        core = self.core if core is None else core
        return (lax.div(y, 2) * 2 + core, lax.rem(y, 2) * 32 + x * 8 + z)

    def sibling(self):
        return self.at(core=1 - self.core)

    def along_z(self, k):
        return self.at(z=lax.rem(self.z + k, NZ))

    def along_y(self, k):
        return self.at(y=lax.rem(self.y + k, NY))

    def along_x(self, k):
        return self.at(x=lax.rem(self.x + k, NX))


def greet(here):
    barrier = pltpu.get_barrier_semaphore()
    friends = [here.along_z(k) for k in range(1, NZ)]
    friends += [here.along_y(k) for k in range(1, NY)] + [here.along_x(k) for k in range(1, NX)]
    friends += [here.sibling()]
    for friend in friends:
        pl.semaphore_signal(barrier, inc=1, device_id=friend, device_id_type=MESH)
    return lambda: pl.semaphore_wait(barrier, len(friends))


def send(src, dst, sems, index, device):
    copy = pltpu.make_async_remote_copy(
        src_ref=src,
        dst_ref=dst,
        send_sem=sems[0].at[index],
        recv_sem=sems[1].at[index],
        device_id=device,
        device_id_type=MESH,
    )
    copy.start()
    return copy


def together(*walks):
    for _ in itertools.zip_longest(*walks):
        pass


GATHER_SEMS = 7 + 3 + 12 + 16


def gather_part(buf, outer, inner, along_outer, along_inner, here, sems, base, landed=None):
    core, z = here.core, here.z
    numbers = itertools.count(base)
    sends, shared, waiting = [], [], []
    plus, minus = along_outer(1), along_outer(3)

    def put(block, device):
        copy = send(block, block, sems, next(numbers), device)
        sends.append(copy)
        return copy

    def report(which, dy, dx):
        if landed is not None:
            landed(which, lax.rem(outer + dy, 4), lax.rem(inner + dx, 4))

    def receive():
        dy, dx, copy = waiting.pop(0)
        copy.wait_recv()
        report(1 - core, dy, dx)

    def share(dy, dx):
        block = spot(dy, dx)
        copy = send(block, block, sems, next(numbers), here.sibling())
        shared.append(copy)
        waiting.append((dy, dx, copy))
        report(core, dy, dx)
        if landed is not None and len(waiting) > 4:
            receive()

    def spot(dy, dx):
        return buf.at[core, lax.rem(outer + dy, 4), lax.rem(inner + dx, 4)]

    mine = buf.at[core, outer, inner, z]
    along_z = [put(mine, here.along_z(k)) for k in (1, 7, 2, 6, 3, 5, 4)]
    yield
    for copy in along_z:
        copy.wait_recv()
    inside = {4 - k: put(spot(0, 0), along_inner(k)) for k in (1, 3, 2)}
    up, down = {0: put(spot(0, 0), plus)}, {0: put(spot(0, 0), minus)}
    share(0, 0)
    onward = []

    def spread(k):
        inside[k].wait_recv()
        up[k], down[k] = put(spot(0, k), plus), put(spot(0, k), minus)
        if k == 2:
            onward.append((k, put(spot(0, k), along_outer(2))))
        share(0, k)

    def from_below(k):
        up[k].wait_recv()
        if k in (0, 3):
            onward.append((k, put(spot(3, k), plus)))
        share(3, k)

    def from_above(k):
        down[k].wait_recv()
        if k == 1:
            onward.append((k, put(spot(1, k), minus)))
        share(1, k)

    yield
    spread(1)
    yield
    spread(3)
    yield
    from_below(0)
    yield
    spread(2)
    for take, k in (
        (from_above, 1),
        (from_below, 3),
        (from_above, 0),
        (from_below, 1),
        (from_above, 3),
        (from_below, 2),
        (from_above, 2),
    ):
        yield
        take(k)
    for k, copy in sorted(onward, key=lambda one: one[0] == 2):
        yield
        copy.wait_recv()
        share(2, k)
    yield
    while waiting:
        receive()
    for copy in sends + shared:
        copy.wait_send()


def gather_walk(buf_a, buf_b, here, sems, landed_a=None, landed_b=None):
    y, x = (here.y, here.along_y), (here.x, here.along_x)
    return itertools.zip_longest(
        gather_part(buf_a, y[0], x[0], y[1], x[1], here, sems, 0, landed_a),
        gather_part(buf_b, x[0], y[0], x[1], y[1], here, sems, GATHER_SEMS, landed_b),
    )


SUM_SEMS = 12 + 3 + 7


def sum_part(total, outer, inner, along_outer, along_inner, bufs, here, sems, base):
    out1, in1, out2, in2, out3, in3 = bufs
    plus, minus = along_outer(1), along_outer(3)
    sends = []

    def block(dy, dx):
        return total.at[lax.rem(outer + dy, 4), lax.rem(inner + dx, 4)]

    def post(out, come, slot, value, device, number):
        out[slot] = value.astype(jnp.bfloat16)
        copy = send(out.at[slot], come.at[slot], sems, base + number, device)
        sends.append(copy)
        return copy

    def ring(slot, value, device):
        return post(out1, in1, slot, value, device, slot)

    def got(come, slot):
        return come[slot].astype(jnp.float32)

    order = (2, 1, 3, 0)
    spots = {k: i for i, k in enumerate(order)}
    up, down = (plus, minus, 1, 3), (minus, plus, 3, 1)
    way = {2: up, 0: up, 1: down, 3: down}
    first, direct, last = {}, {}, {}

    def post_first(k):
        first[k] = ring(spots[k], block(2, k)[...], way[k][0])

    def post_direct(k):
        direct[k] = ring(4 + spots[k], block(way[k][3], k)[...], way[k][1])

    inside = {}

    def finish(i, k):
        last[k].wait_recv()
        direct[k].wait_recv()
        value = block(0, k)[...] + got(in1, 4 + i) + got(in1, 8 + i)
        if k == 0:
            block(0, 0)[...] = value
        else:
            inside[k] = post(out2, in2, k - 1, value, along_inner(k), 11 + k)

    def rest():
        for i, k in enumerate(order):
            yield
            first[k].wait_recv()
            last[k] = ring(8 + i, block(way[k][2], k)[...] + got(in1, i), way[k][0])
        for i, k in enumerate(order):
            yield
            finish(i, k)
        for k in (1, 3, 2):
            yield
            inside[k].wait_recv()
            block(0, 0)[...] = block(0, 0)[...] + got(in2, k - 1)
        along_z = []
        for k in (1, 7, 2, 6, 3, 5, 4):
            value = total[outer, inner, lax.rem(here.z + k, NZ)]
            along_z.append((k, post(out3, in3, k - 1, value, here.along_z(k), 14 + k)))
        yield
        value = total[outer, inner, here.z]
        for k, copy in along_z:
            copy.wait_recv()
            value = value + got(in3, k - 1)
        total[outer, inner, here.z] = value
        for copy in sends:
            copy.wait_send()

    return post_first, post_direct, rest


def part_buffers():
    bf = jnp.bfloat16
    return [
        pltpu.VMEM((12, NZ, ROWS, PART), bf),
        pltpu.VMEM((12, NZ, ROWS, PART), bf),
        pltpu.VMEM((3, NZ, ROWS, PART), bf),
        pltpu.VMEM((3, NZ, ROWS, PART), bf),
        pltpu.VMEM((NZ - 1, ROWS, PART), bf),
        pltpu.VMEM((NZ - 1, ROWS, PART), bf),
    ]


TILE = 256
WIDE = 1024


def one_hot(column, count):
    spots = lax.broadcasted_iota(jnp.int32, (column.shape[0], count), 1).astype(jnp.float32)
    return column == spots


def columns_of(rows):
    return jnp.transpose(rows)


def advantage_of(returns, episode):
    baseline = jnp.zeros_like(returns)
    for number in range(EPI_BLK):
        member = (episode == number).astype(jnp.float32)
        total = jnp.sum(returns * member, keepdims=True)
        count = jnp.sum(member, keepdims=True)
        baseline = baseline + member * (total / count)
    return returns - baseline


def station_rows(rows_ref, tokens, table, gain, mixed, step):
    n = rows_ref.shape[0]
    lookup = one_hot(tokens, STATIONS).astype(jnp.bfloat16)
    power = jnp.zeros((n, 1), jnp.float32)
    for left in range(0, D, WIDE):
        cols = pl.ds(left, WIDE)
        value = rows_ref[:, cols].astype(jnp.float32) + jnp.dot(
            lookup, table[:, cols], preferred_element_type=jnp.float32
        )
        mixed[:n, cols] = value
        power = power + jnp.sum(value * value, axis=-1, keepdims=True)
        step()
    inverse = lax.rsqrt(power * (1.0 / D) + 1e-05)
    for left in range(0, D, WIDE):
        cols = pl.ds(left, WIDE)
        rows_ref[:, cols] = (mixed[:n, cols] * inverse * gain[:, cols]).astype(jnp.bfloat16)
    step()


def whole_kernel(
    hidden_hbm,
    roll_hbm,
    table_hbm,
    gain_hbm,
    tokens_hbm,
    action_hbm,
    roll_tokens_hbm,
    roll_action_hbm,
    returns_hbm,
    episode_hbm,
    shard_hbm,
    new_hbm,
    logp_hbm,
    episode_logp_hbm,
    gain,
    ints,
    roll_ints,
    returns,
    episode,
    shard,
    new_ref,
    logp_ref,
    episode_ref,
    features,
    rollout,
    table,
    mixed,
    scores,
    head,
    squares,
    out0,
    in0,
    total_a,
    total_b,
    *rest,
):
    bufs_a, bufs_b = rest[:6], rest[6:12]
    head_a, head_b, buf_a, buf_b = rest[12:16]
    load_sem, pair_send, pair_recv, sum_send, sum_recv = rest[16:21]
    head_send, head_recv, all_send, all_recv = rest[21:]
    here = Place()
    met = greet(here)

    loads = [pltpu.make_async_copy(table_hbm, table, load_sem.at[0])]
    tiles = [pl.ds(TILE * i, TILE) for i in range(4)]
    for i, rows in enumerate(tiles):
        loads.append(
            pltpu.make_async_copy(hidden_hbm.at[rows], features.at[rows], load_sem.at[1 + i])
        )
    loads.append(pltpu.make_async_copy(roll_hbm, rollout, load_sem.at[5]))
    small = [
        (shard_hbm, shard),
        (tokens_hbm, ints.at[0:8]),
        (action_hbm, ints.at[8:16]),
        (roll_tokens_hbm, roll_ints.at[0]),
        (roll_action_hbm, roll_ints.at[1]),
        (returns_hbm, returns),
        (episode_hbm, episode),
        (gain_hbm, gain),
    ]
    small = [
        pltpu.make_async_copy(src, dst, load_sem.at[6 + i]) for i, (src, dst) in enumerate(small)
    ]
    for load in small:
        load.start()
    loads[0].start()
    loads[1].start()

    small[0].wait()
    rows = pl.ds(pl.multiple_of(here.y_hi * ROWS, ROWS), ROWS)
    for part, (buf, spot) in enumerate(((head_a, (here.y, here.x)), (head_b, (here.x, here.y)))):
        cols = pl.ds(pl.multiple_of(here.core * HALF + part * PART, PART), PART)
        buf[here.core, spot[0], spot[1], here.z] = shard[rows, cols]
    met()
    walk = gather_walk(head_a, head_b, here, (head_send, head_recv))
    next(walk)
    turn = itertools.count(1)

    def step():
        if next(turn) in (6, 9, 10, 11, 12, 13, 14, 15, 16, 17, 18, 19, 20, 21, 22, 23):
            next(walk, None)

    for load in small[1:]:
        load.wait()
    numbers = columns_of(ints[...].astype(jnp.float32))
    beside = jnp.concatenate([roll_ints[0], roll_ints[1]], axis=1).astype(jnp.float32)
    roll_numbers = columns_of(jnp.broadcast_to(beside, (8, 128)))
    advantage = columns_of(advantage_of(returns[...], episode[...]))

    def column(values, first, tile):
        return jnp.concatenate([values[:, first + 2 * tile + j][:, None] for j in range(2)], axis=0)

    loads[0].wait()
    for i, rows in enumerate(tiles):
        loads[2 + i].start()
        loads[1 + i].wait()
        station_rows(features.at[rows], column(numbers, 0, i), table, gain, mixed, step)
    loads[5].wait()
    station_rows(rollout, roll_numbers[:STEPS, :1], table, gain, mixed, step)
    for _ in walk:
        pass
    for core, y, x in itertools.product(range(2), range(NY), range(NX)):
        for part, blocks in enumerate((head_a[core, y, x], head_b[core, x, y])):
            head[y % 2, x, :, y // 2, :, pl.ds(core * HALF + part * PART, PART)] = blocks

    for i, rows in enumerate(tiles):
        logits = jnp.dot(
            features[rows, :],
            head[...].reshape(D, ACTIONS),
            preferred_element_type=jnp.float32,
        )
        expo = jnp.exp(logits - jnp.max(logits, axis=-1, keepdims=True))
        probs = expo / jnp.sum(expo, axis=-1, keepdims=True)
        chosen = one_hot(column(numbers, 8, i), ACTIONS).astype(jnp.float32)
        value = (column(advantage, 0, i) * (probs - chosen)).astype(jnp.bfloat16)
        scores[0, rows] = value[:, :HALF]
        scores[1, rows] = value[:, HALF:]

    sems = (sum_send, sum_recv)
    first_a, direct_a, rest_a = sum_part(
        total_a, here.y, here.x, here.along_y, here.along_x, bufs_a, here, sems, 0
    )
    first_b, direct_b, rest_b = sum_part(
        total_b, here.x, here.y, here.along_x, here.along_y, bufs_b, here, sems, SUM_SEMS
    )
    pairs = []
    mine, theirs = scores[here.core], scores[1 - here.core]

    def chunk(far, dx):
        y_lo = lax.rem(here.y + far, 2)
        return y_lo, lax.rem(here.x + dx, NX)

    def make(far, dx):
        y_lo, x = chunk(far, dx)
        cols = pl.ds(pl.multiple_of(y_lo * (D // 2) + x * 512, 512), 512)
        left = jnp.transpose(features[:, cols])
        k = len(pairs)
        out0[k] = jnp.dot(left, theirs, preferred_element_type=jnp.float32).astype(jnp.bfloat16)
        pairs.append(send(out0.at[k], in0.at[k], (pair_send, pair_recv), k, here.sibling()))
        own = jnp.dot(left, mine, preferred_element_type=jnp.float32).reshape(NZ, 2, ROWS, HALF)
        for y_hi in range(2):
            total_a[2 * y_hi + y_lo, x] = own[:, y_hi, :, :PART]
            total_b[x, 2 * y_hi + y_lo] = own[:, y_hi, :, PART:]

    def both(k, far, dx):
        y_lo, x = chunk(far, dx)
        pairs[k].wait_recv()
        other = in0[k].astype(jnp.float32).reshape(NZ, 2, ROWS, HALF)
        for y_hi in range(2):
            y = 2 * y_hi + y_lo
            total_a[y, x] = total_a[y, x] + other[:, y_hi, :, :PART]
            total_b[x, y] = total_b[x, y] + other[:, y_hi, :, PART:]

    ready = [
        ((0, 2), [(first_b, 2), (first_a, 2), (first_b, 0)]),
        ((1, 2), [(first_b, 1), (first_b, 3), (direct_a, 2)]),
        ((0, 1), [(first_a, 1)]),
        ((0, 3), [(first_a, 3), (direct_b, 2), (direct_b, 0)]),
        ((0, 0), [(first_a, 0)]),
        ((1, 1), [(direct_a, 1), (direct_b, 1), (direct_b, 3)]),
        ((1, 3), [(direct_a, 3)]),
        ((1, 0), [(direct_a, 0)]),
    ]

    def settle(k):
        both(k, *ready[k][0])
        for post, distance in ready[k][1]:
            post(distance)

    summing = itertools.zip_longest(rest_a(), rest_b())
    next(summing)
    for k, (where, _) in enumerate(ready):
        make(*where)
        if k:
            settle(k - 1)
        if k >= 6:
            next(summing)
    settle(7)
    for copy in pairs:
        copy.wait_send()

    for turn, _ in enumerate(summing):
        if turn == 8:
            mixed[:STEPS, :ACTIONS] = jnp.dot(
                rollout[...], head[...].reshape(D, ACTIONS), preferred_element_type=jnp.float32
            )
            shard[...] = head[lax.rem(here.y, 2), here.x, here.z].reshape(2 * ROWS, ACTIONS)

    buf_a[here.core, here.y, here.x, here.z] = total_a[here.y, here.x, here.z].astype(jnp.bfloat16)
    buf_b[here.core, here.x, here.y, here.z] = total_b[here.x, here.y, here.z].astype(jnp.bfloat16)

    def landing(part, buf, y_first):
        def landed(core, a, b):
            y, x = (a, b) if y_first else (b, a)
            block = buf[core, a, b]
            cols = pl.ds(pl.multiple_of(core * HALF + part * PART, PART), PART)
            head[lax.rem(y, 2), x, :, lax.div(y, 2), :, cols] = block
            block = block.astype(jnp.float32)
            squares[core, part, y, x] = jnp.sum((block * block).reshape(-1, 8, PART), axis=0)

        return landed

    for _ in gather_walk(
        buf_a,
        buf_b,
        here,
        (all_send, all_recv),
        landing(0, buf_a, True),
        landing(1, buf_b, False),
    ):
        pass

    scale = step_length * lax.rsqrt(jnp.sum(squares[...], keepdims=True).reshape(1, 1) + 1e-06)
    change = head[lax.rem(here.y, 2), here.x, here.z].reshape(2 * ROWS, ACTIONS)
    new_ref[...] = (
        shard[...].astype(jnp.float32) - change.astype(jnp.float32) * scale
    ).astype(jnp.bfloat16)
    new_store = pltpu.make_async_copy(new_ref, new_hbm, load_sem.at[2])
    new_store.start()
    logits = mixed[:STEPS, :ACTIONS] - scale * jnp.dot(
        rollout[...], head[...].reshape(D, ACTIONS), preferred_element_type=jnp.float32
    )
    top = jnp.max(logits, axis=-1, keepdims=True)
    total = jnp.log(jnp.sum(jnp.exp(logits - top), axis=-1, keepdims=True)) + top
    chosen = one_hot(roll_numbers[STEPS:, :1], ACTIONS).astype(jnp.float32)
    logp = jnp.sum(logits * chosen, axis=-1, keepdims=True) - total
    logp_ref[...] = jnp.transpose(jnp.broadcast_to(logp, (STEPS, 128)))[:1, :]
    episode_ref[...] = jnp.broadcast_to(jnp.sum(logp, keepdims=True), (1, 128))
    stores = [
        pltpu.make_async_copy(src, dst, load_sem.at[i])
        for i, (src, dst) in enumerate(((logp_ref, logp_hbm), (episode_ref, episode_logp_hbm)))
    ]
    for store in stores:
        store.start()
    for store in stores + [new_store]:
        store.wait()


SPREAD = (2, NX, NZ, 2, ROWS, ACTIONS)


def dma_sems(count):
    return [pltpu.SemaphoreType.DMA((count,)), pltpu.SemaphoreType.DMA((count,))]


def gather_buffers():
    return [
        pltpu.VMEM((2, NY, NX, NZ, ROWS, PART), jnp.bfloat16),
        pltpu.VMEM((2, NX, NY, NZ, ROWS, PART), jnp.bfloat16),
    ]


def hand_over(*refs):
    for source, target in zip(refs[:3], refs[3:]):
        target[...] = source[...]


def results(*arrays):
    vmem = pl.BlockSpec(memory_space=pltpu.VMEM)
    return pl.pallas_call(
        hand_over,
        out_shape=tuple(jax.ShapeDtypeStruct(a.shape, a.dtype) for a in arrays),
        in_specs=[vmem] * 3,
        out_specs=(vmem,) * 3,
    )(*arrays)


def whole_step(*arrays):
    anywhere = pl.BlockSpec(memory_space=pl.ANY)
    return pl.pallas_call(
        whole_kernel,
        out_shape=(
            jax.ShapeDtypeStruct((2 * ROWS, ACTIONS), jnp.bfloat16),
            jax.ShapeDtypeStruct((1, STEPS), jnp.float32),
            jax.ShapeDtypeStruct((1, 128), jnp.float32),
        ),
        in_specs=[anywhere] * len(arrays),
        out_specs=(anywhere,) * 3,
        scratch_shapes=[
            pltpu.VMEM((1, D), jnp.float32),
            pltpu.VMEM((16, 128), jnp.int32),
            pltpu.VMEM((2, 1, STEPS), jnp.int32),
            pltpu.VMEM((8, 128), jnp.float32),
            pltpu.VMEM((8, 128), jnp.int32),
            pltpu.VMEM((2 * ROWS, ACTIONS), jnp.bfloat16),
            pltpu.VMEM((2 * ROWS, ACTIONS), jnp.bfloat16),
            pltpu.VMEM((1, STEPS), jnp.float32),
            pltpu.VMEM((1, 128), jnp.float32),
            pltpu.VMEM((1024, D), jnp.bfloat16),
            pltpu.VMEM((STEPS, D), jnp.bfloat16),
            pltpu.VMEM((STATIONS, D), jnp.bfloat16),
            pltpu.VMEM((TILE, D), jnp.float32),
            pltpu.VMEM((2, 1024, HALF), jnp.bfloat16),
            pltpu.VMEM(SPREAD, jnp.bfloat16),
            pltpu.VMEM((2, 2, NY, NX, 8, PART), jnp.float32),
            pltpu.VMEM((8, 512, HALF), jnp.bfloat16),
            pltpu.VMEM((8, 512, HALF), jnp.bfloat16),
            pltpu.VMEM((NY, NX, NZ, ROWS, PART), jnp.float32),
            pltpu.VMEM((NX, NY, NZ, ROWS, PART), jnp.float32),
            *part_buffers(),
            *part_buffers(),
            *gather_buffers(),
            *gather_buffers(),
            pltpu.SemaphoreType.DMA((14,)),
            *dma_sems(8),
            *dma_sems(2 * SUM_SEMS),
            *dma_sems(2 * GATHER_SEMS),
            *dma_sems(2 * GATHER_SEMS),
        ],
        compiler_params=pltpu.CompilerParams(
            collective_id=0, has_side_effects=True, vmem_limit_bytes=60 << 20
        ),
    )(*arrays)


def local(
    traj_hidden,
    traj_tokens,
    traj_action,
    traj_return,
    traj_episode,
    roll_hidden,
    roll_tokens,
    roll_action,
    station_table,
    norm_gain,
    head_weight,
):
    arrays = whole_step(
        traj_hidden,
        roll_hidden,
        station_table,
        norm_gain.reshape(1, D),
        traj_tokens.reshape(8, 128),
        traj_action.reshape(8, 128),
        roll_tokens.reshape(1, STEPS),
        roll_action.reshape(1, STEPS),
        traj_return.reshape(8, 128),
        traj_episode.reshape(8, 128),
        head_weight,
    )
    new_head, action_logp, episode_logp = results(*arrays)
    return (new_head, action_logp.reshape(STEPS), episode_logp[0, :1])


def solution(mesh):
    placed = (
        P(("grp", "fsdp"), None),
        P(("grp", "fsdp")),
        P(("grp", "fsdp")),
        P(("grp", "fsdp")),
        P(("grp", "fsdp"), None),
        P(("grp", "fsdp"), None),
        P(("grp", "fsdp")),
        P(("grp", "fsdp")),
        P(),
        P(),
        P("fsdp", None),
    )
    return jax.shard_map(
        local,
        mesh=mesh,
        in_specs=placed,
        out_specs=(P("fsdp", None), P(("grp", "fsdp")), P(("grp", "fsdp"))),
        check_vma=False,
    )
```
